32 devices in a mesh: dp: 4 (over z), seq: 8 (over y, x, core).
Axes of the slice: x: 2, y: 2, z: 4, core: 2. Of those that a mesh axis runs over, the one named last changes fastest.
Arguments:
- tokens: bfloat16 [4, 4096, 256], P('dp', 'seq'), may hold values from -6 to 6
- cotangent: bfloat16 [4, 4096, 256], P('dp', 'seq'), may hold values from -6 to 6
- w_in: bfloat16 [256, 768], replicated, may hold values from -0.375 to 0.375
- w_out: bfloat16 [256, 256], replicated, may hold values from -0.375 to 0.375
- filter_taps: float32 [4096, 256], P('seq'), may hold values from -0.09375 to 0.09375
- skip: float32 [256], replicated, may hold values from -4 to 4
Outputs:
- output: bfloat16 [4, 4096, 256], P('dp', 'seq')
- dinput: bfloat16 [4, 4096, 256], P('dp', 'seq')
- grad_in_proj: float32 [256, 768], P('dp')
- grad_out_proj: float32 [256, 256], P('dp')
- grad_filter: float32 [4096, 256], P('seq', 'dp')
- grad_skip: float32 [256], P('dp')
The draws below stay inside these ranges and needn't reach their ends.
All inputs are finite; a program needn't handle non-finite values.
Results may differ from the reference program's by a relative error of at most 0.0049.
Values sent between devices are 32-bit elements; how exact they have to be, the bound alone decides.
No kernel may reach another device: no remote copies, remote signals or barrier semaphores. Data moves between devices by JAX's collectives and lax.ppermute only.
A program may use at most 128 MiB of HBM per device.

```python
import math
import jax
import jax.numpy as jnp
from jax import lax

D = 256
SEQS = 4
LENGTH = 4096


def shard_levels(key, shape, pieces, least, top_value):
    factor_of, own = 1.0, jax.random.fold_in(key, 6)
    for dim, blocks in pieces:
        steps = jnp.exp(jax.random.uniform(jax.random.fold_in(own, dim), (blocks,), jnp.float32, least / len(pieces), top_value / len(pieces)))
        factor_of = factor_of * jnp.repeat(steps, shape[dim] // blocks).reshape([-1 if axis == dim else 1 for axis in range(len(shape))])
    return factor_of


def centred(stream_key, shape, deviation, bound, split=(), held_as=jnp.bfloat16):
    factor_of = shard_levels(stream_key, shape, split, -0.22, 0.18) if split else 1.0
    drawn = jax.random.normal(stream_key, shape, jnp.float32) * deviation * factor_of
    return jnp.minimum(jnp.maximum(drawn, -bound), bound).astype(held_as)


def setup_inputs(seed: int = 0) -> dict:
    streams_of = jax.random.split(jax.random.key(seed), 7)
    return {
        "tokens": centred(streams_of[0], (SEQS, LENGTH, D), 1.0, 6.0, ((0, 4), (1, 8))),
        "cotangent": centred(streams_of[1], (SEQS, LENGTH, D), 1.0, 6.0, ((0, 4), (1, 8))),
        "w_in": centred(streams_of[2], (D, 3 * D), D ** -0.5, 0.375),
        "w_out": centred(streams_of[3], (D, D), D ** -0.5, 0.375),
        "filter_taps": centred(streams_of[4], (LENGTH, D), LENGTH ** -0.5, 0.09375, ((0, 8),), jnp.float32),
        "skip": centred(streams_of[5], (D,), 1.0, 4.0, (), jnp.float32),
    }


def reference(tokens, cotangent, w_in, w_out, filter_taps, skip):
    model_width = w_out.shape[0]
    seq_length = tokens.shape[1]
    padded = 2 * seq_length
    taps_spec = jnp.fft.rfft(filter_taps, n=padded, axis=0)

    def one_sequence(carry, pair):
        seq_in, grad_out = pair
        projected = jnp.dot(seq_in, w_in, preferred_element_type=jnp.float32)
        gate_out = projected[:, :model_width]
        gate_in = projected[:, model_width:2 * model_width]
        values = projected[:, 2 * model_width:]
        gated = values * gate_in
        gated_spec = jnp.fft.rfft(gated, n=padded, axis=0)
        conv = jnp.fft.irfft(gated_spec * taps_spec, n=padded, axis=0)[:seq_length] + skip * gated
        mixed = (conv * gate_out).astype(jnp.bfloat16)
        output = jnp.dot(mixed, w_out, preferred_element_type=jnp.float32).astype(jnp.bfloat16)
        dmixed = jnp.dot(grad_out, w_out.T, preferred_element_type=jnp.float32)
        dconv = dmixed * gate_out
        dconv_spec = jnp.fft.rfft(dconv, n=padded, axis=0)
        dgated = jnp.fft.irfft(jnp.conj(taps_spec) * dconv_spec, n=padded, axis=0)[:seq_length] + skip * dconv
        taps_term = jnp.fft.irfft(jnp.conj(gated_spec) * dconv_spec, n=padded, axis=0)[:seq_length]
        dproj = jnp.concatenate([dmixed * conv, dgated * values, dgated * gate_in], axis=1).astype(jnp.bfloat16)
        dinput = jnp.dot(dproj, w_in.T, preferred_element_type=jnp.float32).astype(jnp.bfloat16)
        in_term = jnp.dot(seq_in.T, dproj, preferred_element_type=jnp.float32)
        out_term = jnp.dot(mixed.T, grad_out, preferred_element_type=jnp.float32)
        skip_term = lax.optimization_barrier(jnp.sum(dconv * gated, axis=0))
        in_acc, out_acc, taps_acc, skip_acc = carry
        return ((in_acc + in_term, out_acc + out_term, taps_acc + taps_term, skip_acc + skip_term), (output, dinput))
    start = (jnp.zeros((model_width, 3 * model_width), jnp.float32), jnp.zeros((model_width, model_width), jnp.float32), jnp.zeros((seq_length, model_width), jnp.float32), jnp.zeros((model_width,), jnp.float32))
    totals, stacked = lax.scan(one_sequence, start, (tokens, cotangent))
    grad_scale = 1.0 / math.sqrt(tokens.shape[0] * seq_length)
    return (stacked[0], stacked[1], totals[0] * grad_scale, totals[1] * grad_scale, totals[2] * grad_scale, totals[3] * grad_scale)
```

```python
import math

import jax
import jax.numpy as jnp
import numpy as np
from jax import lax
from jax.experimental import pallas as pl
from jax.experimental.pallas import tpu as pltpu
from jax.sharding import PartitionSpec as P

LANES = 128
F32 = jnp.float32
BF16 = jnp.bfloat16
SHIFT = 0.25


def split_const(table):
    high = table.astype(BF16)
    low = (table - high.astype(np.float64)).astype(BF16)
    return high, low


def tables(seq_parts, tiles):
    outer = seq_parts * tiles
    length = outer * LANES
    row = np.arange(outer)
    row_pos = (row % seq_parts) * tiles + row // seq_parts
    freq = np.arange(outer) + SHIFT
    lane = np.arange(LANES)
    angle = 2.0 * np.pi * np.outer(freq, row_pos) / outer
    fwd_high, fwd_low = split_const(np.concatenate([np.cos(angle), -np.sin(angle)], axis=0))
    first = np.concatenate([fwd_high, fwd_high, fwd_low], axis=1)
    inv_high, inv_low = split_const(
        np.concatenate([np.cos(angle.T), -np.sin(angle.T)], axis=1) / length
    )
    last = np.concatenate([inv_high, inv_high, inv_low], axis=1)
    turn = 2.0 * np.pi * np.outer(freq, lane) / length
    twiddle = np.stack([np.cos(turn), -np.sin(turn)]).astype(np.float32)
    inner = 2.0 * np.pi * np.outer(lane, lane) / LANES
    cos, sin = np.cos(inner), np.sin(inner)
    wide_fwd = np.stack(split_const(np.block([[cos, -sin], [sin, cos]])))
    wide_inv = np.stack(split_const(np.block([[cos, sin], [-sin, cos]])))
    return [jnp.asarray(t) for t in (first, last, twiddle, wide_fwd, wide_inv)]


def dot(a, b, contract=((1,), (0,))):
    return lax.dot_general(a, b, (contract, ((), ())), preferred_element_type=F32)


def split(x):
    high = x.astype(BF16)
    return high, (x - high.astype(F32)).astype(BF16)


def projections(tok_ref, cot_ref, win_ref, wout_ref):
    width = wout_ref.shape[0]
    projected = dot(win_ref[...], tok_ref[...], ((0,), (1,)))
    dmixed = dot(wout_ref[...], cot_ref[...], ((1,), (1,)))
    return projected[:width], projected[width : 2 * width], projected[2 * width :], dmixed


def prep_kernel(tok_ref, cot_ref, win_ref, wout_ref, taps_ref, send_ref):
    parts, _, tiles, chans, _ = send_ref.shape
    gate_out, gate_in, values, dmixed = projections(tok_ref, cot_ref, win_ref, wout_ref)
    signals = (values * gate_in, dmixed * gate_out, taps_ref[...].T)
    for sig, signal in enumerate(signals):
        for dest in range(parts):
            for tile in range(tiles):
                send_ref[dest, sig, tile] = signal[
                    dest * chans : (dest + 1) * chans, tile * LANES : (tile + 1) * LANES
                ]


def conv_kernel(parts, tiles, chans, chunk, recv_ref, first_ref, last_ref, tw_ref, fwd_ref, inv_ref, out_ref, zh_ref, zl_ref):
    outer = parts * tiles
    stride = 3 * tiles * chans
    tw_re, tw_im = tw_ref[0], tw_ref[1]

    def rows(sig, tile, chan):
        return pl.ds(sig * tiles * chans + tile * chans + chan, parts, stride=stride)

    def wide(high, low, ref):
        return dot(high, ref[0]) + dot(low, ref[0]) + dot(high, ref[1])

    def load(sig, chan):
        return jnp.concatenate([recv_ref[rows(sig, t, chan), :] for t in range(tiles)], axis=0)

    def step(index, _):
        base = index * chunk
        spectra = []
        for sig in range(3):
            for pair in range(chunk // 2):
                chan = base + 2 * pair
                x = jnp.concatenate([load(sig, chan), load(sig, chan + 1)], axis=1)
                high, low = split(x)
                a = dot(first_ref[...], jnp.concatenate([high, low, high], axis=0))
                for side in range(2):
                    lanes = slice(side * LANES, (side + 1) * LANES)
                    re, im = a[:outer, lanes], a[outer:, lanes]
                    z = jnp.concatenate(
                        [re * tw_re - im * tw_im, re * tw_im + im * tw_re], axis=1
                    )
                    high, low = split(z)
                    place = pl.ds((2 * pair + side) * outer, outer)
                    zh_ref[sig, place, :] = high
                    zl_ref[sig, place, :] = low
            f = wide(zh_ref[sig], zl_ref[sig], fwd_ref)
            spectra.append((f[:, :LANES], f[:, LANES:]))
        (g_re, g_im), (d_re, d_im), (h_re, h_im) = spectra
        products = (
            (h_re * g_re - h_im * g_im, h_re * g_im + h_im * g_re),
            (h_re * d_re + h_im * d_im, h_re * d_im - h_im * d_re),
            (g_re * d_re + g_im * d_im, g_re * d_im - g_im * d_re),
        )
        for sig, (re, im) in enumerate(products):
            high, low = split(jnp.concatenate([re, im], axis=1))
            u = wide(high, low, inv_ref)
            for pair in range(chunk // 2):
                sides = []
                for side in range(2):
                    start = (2 * pair + side) * outer
                    u_re, u_im = u[start : start + outer, :LANES], u[start : start + outer, LANES:]
                    sides.append(
                        jnp.concatenate(
                            [u_re * tw_re + u_im * tw_im, u_im * tw_re - u_re * tw_im], axis=0
                        )
                    )
                high, low = split(jnp.concatenate(sides, axis=1))
                y = dot(last_ref[...], jnp.concatenate([high, low, high], axis=0))
                for side in range(2):
                    chan = base + 2 * pair + side
                    for t in range(tiles):
                        out_ref[rows(sig, t, chan), :] = y[
                            t * parts : (t + 1) * parts, side * LANES : (side + 1) * LANES
                        ]
        return 0

    lax.fori_loop(0, chans // chunk, step, 0)


def final_kernel(scale, tok_ref, cot_ref, win_ref, wout_ref, skip_ref, back_ref, out_ref, din_ref, part_ref):
    parts, _, tiles, chans, _ = back_ref.shape
    width = wout_ref.shape[0]
    gate_out, gate_in, values, dmixed = projections(tok_ref, cot_ref, win_ref, wout_ref)
    gated = values * gate_in
    dconv = dmixed * gate_out

    def gather(sig):
        return jnp.concatenate(
            [
                jnp.concatenate([back_ref[src, sig, t] for t in range(tiles)], axis=1)
                for src in range(parts)
            ],
            axis=0,
        )

    skip = skip_ref[...]
    conv = gather(0) + skip * gated
    dgated = gather(1) + skip * dconv
    mixed = (conv * gate_out).astype(BF16)
    dproj = jnp.concatenate(
        [(dmixed * conv).astype(BF16), (dgated * values).astype(BF16), (dgated * gate_in).astype(BF16)],
        axis=0,
    )
    out_ref[...] = dot(mixed, wout_ref[...], ((0,), (0,))).astype(BF16)
    din_ref[...] = dot(dproj, win_ref[...], ((0,), (1,))).astype(BF16)
    part_ref[:, : 3 * width] = dot(tok_ref[...], dproj, ((0,), (1,))) * scale
    part_ref[:, 3 * width : 4 * width] = dot(mixed, cot_ref[...]) * scale
    product = dconv * gated * scale
    total = product[:, :LANES]
    for t in range(1, tiles):
        total = total + product[:, t * LANES : (t + 1) * LANES]
    part_ref[:, 4 * width :] = total


def exchange(x, axis):
    return lax.all_to_all(x, axis, split_axis=0, concat_axis=0, tiled=True)


def shards(tokens, cotangent, w_in, w_out, filter_taps, skip):
    width = w_out.shape[0]
    tok, cot = tokens[0], cotangent[0]
    rows = tok.shape[0]
    tiles = rows // LANES
    parts = lax.axis_size("seq")
    groups = lax.axis_size("dp")
    chans = width // parts
    outer = parts * tiles
    chunk = min(chans, 8)
    scale = 1.0 / math.sqrt(groups * parts * rows)
    first, last, twiddle, fwd, inv = tables(parts, tiles)
    shape = (parts, 3, tiles, chans, LANES)

    send = pl.pallas_call(
        prep_kernel,
        out_shape=jax.ShapeDtypeStruct(shape, F32),
        name="prep",
    )(tok, cot, w_in, w_out, filter_taps)
    recv = exchange(send, "seq")
    flat = (parts * 3 * tiles * chans, LANES)

    def body(*refs):
        conv_kernel(parts, tiles, chans, chunk, *refs)

    fields = pl.pallas_call(
        body,
        out_shape=jax.ShapeDtypeStruct(flat, F32),
        scratch_shapes=[pltpu.VMEM((3, chunk * outer, 2 * LANES), BF16)] * 2,
        name="convolve",
    )(recv.reshape(flat), first, last, twiddle, fwd, inv)
    back = exchange(fields.reshape(shape), "seq")

    def tail(*refs):
        final_kernel(scale, *refs)

    output, dinput, part = pl.pallas_call(
        tail,
        out_shape=(
            jax.ShapeDtypeStruct((rows, width), BF16),
            jax.ShapeDtypeStruct((rows, width), BF16),
            jax.ShapeDtypeStruct((width, 4 * width + LANES), F32),
        ),
        name="finish",
    )(tok, cot, w_in, w_out, skip[:, None], back)

    share = parts // groups
    taps = exchange(back[:, 2], "dp").reshape(groups, share, tiles, chans, LANES)
    taps = jnp.sum(taps, axis=0) * scale
    taps_part = taps.transpose(1, 3, 0, 2).reshape(rows, share * chans)

    cols = part.shape[1]
    piece = width // (groups * parts)
    part = part.reshape(groups, parts, piece, cols).transpose(1, 0, 2, 3)
    part = jnp.sum(exchange(part, "seq").reshape(parts, groups, piece, cols), axis=0)
    part = jnp.sum(exchange(part, "dp").reshape(groups, piece, cols), axis=0)
    spread = jnp.broadcast_to(part[None], (parts, piece, cols))
    total = exchange(spread, "seq").reshape(parts * piece, cols)
    return (
        output[None],
        dinput[None],
        total[:, : 3 * width],
        total[:, 3 * width : 4 * width],
        taps_part,
        jnp.sum(total[:, 4 * width :], axis=1),
    )


def solution(mesh):
    return jax.shard_map(
        shards,
        mesh=mesh,
        in_specs=(P("dp", "seq", None), P("dp", "seq", None), P(), P(), P("seq", None), P()),
        out_specs=(
            P("dp", "seq", None),
            P("dp", "seq", None),
            P("dp", None),
            P("dp", None),
            P("seq", "dp"),
            P("dp"),
        ),
        check_vma=False,
    )
```

```python
import math

import jax
import jax.numpy as jnp
import numpy as np
from jax import lax
from jax.experimental import pallas as pl
from jax.experimental.pallas import tpu as pltpu
from jax.sharding import PartitionSpec as P


LANES = 128
F32 = jnp.float32
BF16 = jnp.bfloat16
SHIFT = 0.25
VMEM_GRANT = 8 * 2**20
PREP_GRANT = 54984704


def split_const(table):
    high = table.astype(BF16)
    low = (table - high.astype(np.float64)).astype(BF16)
    return high, low


def tables(outer):
    length = outer * LANES
    place = np.arange(outer)
    freq = place + SHIFT
    lane = np.arange(LANES)
    angle = 2.0 * np.pi * np.outer(freq, place) / outer
    high, low = split_const(np.concatenate([np.cos(angle), -np.sin(angle)], axis=0))
    first = np.concatenate([high, high, low], axis=1)
    back = np.concatenate([np.cos(angle.T), -np.sin(angle.T)], axis=1) / length
    high, low = split_const(back)
    last = np.concatenate([high, high, low], axis=1)
    turn = 2.0 * np.pi * np.outer(freq, lane) / length
    twiddle = np.stack([np.cos(turn), -np.sin(turn)]).astype(np.float32)
    inner = 2.0 * np.pi * np.outer(lane, lane) / LANES
    cos, sin = np.cos(inner), np.sin(inner)
    fwd = np.stack(split_const(np.block([[cos, -sin], [sin, cos]])))
    inv = np.stack(split_const(np.block([[cos, sin], [-sin, cos]])))
    return [jnp.asarray(t) for t in (first, last, twiddle, fwd, inv)]


def dot(a, b, contract=((1,), (0,))):
    return lax.dot_general(a, b, (contract, ((), ())), preferred_element_type=F32)


def split(x):
    high = x.astype(BF16)
    return high, (x - high.astype(F32)).astype(BF16)


def wide(high, low, ref):
    return dot(high, ref[0]) + dot(low, ref[0]) + dot(high, ref[1])


def multiply(a, b):
    return a[0] * b[0] - a[1] * b[1], a[0] * b[1] + a[1] * b[0]


def correlate(a, b):
    return a[0] * b[0] + a[1] * b[1], a[0] * b[1] - a[1] * b[0]


def halves(x):
    return x[:, :LANES], x[:, LANES:]


def projections(tok_ref, cot_ref, win_ref, wout_ref):
    width = wout_ref.shape[0]
    projected = dot(win_ref[...], tok_ref[...], ((0,), (1,)))
    dmixed = dot(wout_ref[...], cot_ref[...], ((1,), (1,)))
    return projected[:width], projected[width : 2 * width], projected[2 * width :], dmixed


def skip_column(skip_ref, tiles):
    column = jnp.broadcast_to(skip_ref[...], (LANES, skip_ref.shape[1])).T
    return jnp.concatenate([column] * tiles, axis=1)


def deal(me, signal_ref, keep_ref, give_ref):
    count, size, _ = keep_ref.shape
    tiles = signal_ref.shape[1] // LANES
    chans = size // tiles
    for k in range(count):
        for flip, ref in enumerate((keep_ref, give_ref)):
            dest = me ^ (2 * k + flip)
            start = pl.multiple_of(dest * chans, chans)
            for t in range(tiles):
                ref[k, t * chans : (t + 1) * chans, :] = signal_ref[
                    pl.ds(start, chans), t * LANES : (t + 1) * LANES
                ]


def blocks_of(me, keep_ref, got_ref, recv_refs):
    yield me, keep_ref.at[0]
    yield me ^ 1, got_ref.at[0]
    for k, ref in enumerate(recv_refs):
        for flip in range(2):
            yield me ^ (2 * (k + 1) + flip), ref.at[flip]


def collect(me, field_ref, blocks):
    for source, ref in blocks_of(me, *blocks):
        size = ref.shape[0]
        field_ref[pl.ds(pl.multiple_of(source * size, size), size), :] = ref[...]


def collect_signal(me, signal_ref, blocks):
    tiles = signal_ref.shape[1] // LANES
    for source, ref in blocks_of(me, *blocks):
        chans = ref.shape[0] // tiles
        start = pl.multiple_of(source * chans, chans)
        for t in range(tiles):
            signal_ref[pl.ds(start, chans), t * LANES : (t + 1) * LANES] = ref[
                t * chans : (t + 1) * chans, :
            ]


def deal_field(me, field_ref, keep_ref, give_ref):
    count, size, _ = keep_ref.shape
    for k in range(count):
        for flip, ref in enumerate((keep_ref, give_ref)):
            dest = me ^ (2 * k + flip)
            ref[k] = field_ref[pl.ds(pl.multiple_of(dest * size, size), size), :]


def forward(field_ref, base, chunk, chans, first_ref, tw_ref, fwd_ref, zh_ref, zl_ref):
    outer = tw_ref.shape[1]
    tw_re, tw_im = tw_ref[0], tw_ref[1]
    for pair in range(chunk // 2):
        chan = base + 2 * pair
        x = jnp.concatenate(
            [field_ref[pl.ds(chan + side, outer, stride=chans), :] for side in range(2)], axis=1
        )
        high, low = split(x)
        a = dot(first_ref[...], jnp.concatenate([high, low, high], axis=0))
        for side in range(2):
            lanes = slice(side * LANES, (side + 1) * LANES)
            re, im = a[:outer, lanes], a[outer:, lanes]
            z = jnp.concatenate([re * tw_re - im * tw_im, re * tw_im + im * tw_re], axis=1)
            place = slice((2 * pair + side) * outer, (2 * pair + side + 1) * outer)
            zh_ref[place, :], zl_ref[place, :] = split(z)
    return wide(zh_ref[...], zl_ref[...], fwd_ref)


def inverse(pair_of, field_ref, base, chunk, chans, last_ref, tw_ref, inv_ref):
    outer = tw_ref.shape[1]
    tw_re, tw_im = tw_ref[0], tw_ref[1]
    high, low = split(jnp.concatenate(pair_of, axis=1))
    u = wide(high, low, inv_ref)
    for pair in range(chunk // 2):
        sides = []
        for side in range(2):
            start = (2 * pair + side) * outer
            re, im = halves(u[start : start + outer])
            sides.append(jnp.concatenate([re * tw_re + im * tw_im, im * tw_re - re * tw_im], axis=0))
        high, low = split(jnp.concatenate(sides, axis=1))
        y = dot(last_ref[...], jnp.concatenate([high, low, high], axis=0))
        for side in range(2):
            chan = base + 2 * pair + side
            field_ref[pl.ds(chan, outer, stride=chans), :] = y[:, side * LANES : (side + 1) * LANES]


def call(body, operands, outs, scratch=(), flops=0, space=pltpu.VMEM, grant=VMEM_GRANT):
    size = sum(x.size * x.dtype.itemsize for x in list(operands) + list(outs))
    specs = [pl.BlockSpec(memory_space=pltpu.SMEM)]
    specs += [pl.BlockSpec(memory_space=space)] * (len(operands) - 1)
    return pl.pallas_call(
        body,
        out_shape=tuple(outs),
        in_specs=specs,
        out_specs=tuple(pl.BlockSpec(memory_space=pltpu.VMEM) for _ in outs),
        scratch_shapes=list(scratch),
        cost_estimate=pl.CostEstimate(flops=flops, bytes_accessed=size, transcendentals=0),
        compiler_params=pltpu.CompilerParams(vmem_limit_bytes=grant),
    )(*operands)


def mirror(x, axis, mask):
    count = lax.axis_size(axis)
    return lax.ppermute(x, axis, [(i, i ^ mask) for i in range(count)])


def exchange(keep, give):
    got = mirror(give, "seq", 1)
    recv = []
    for k in range(1, keep.shape[0]):
        both = jnp.stack([keep[k], got[k]])
        recv.append(mirror(both, "seq", 2 * k))
    return [keep, got] + recv


def tree_sum(terms):
    while len(terms) > 1:
        terms = [a + b for a, b in zip(terms[::2], terms[1::2])]
    return terms[0]


def reversed_bits(slot, count):
    value = 0
    while count > 1:
        value = 2 * value + slot % 2
        slot //= 2
        count //= 2
    return value


def halve(x):
    mask = 1
    while x.shape[0] > 1:
        middle = x.shape[0] // 2
        x = x[:middle] + mirror(x[middle:], "dp", mask)
        mask *= 2
    return x[0]


def reduce_rows(keep, give):
    return halve(keep + mirror(give, "seq", 1))


def spread_rows(held):
    whole = [held]
    for k in range(1, lax.axis_size("seq") // 2):
        whole.append(mirror(held, "seq", 2 * k))
    whole = tree_sum(whole)
    return whole, mirror(whole, "seq", 1)


def shards(tokens, cotangent, w_in, w_out, filter_taps, skip):
    width = w_out.shape[0]
    tok, cot = tokens[0], cotangent[0]
    rows = tok.shape[0]
    tiles = rows // LANES
    parts = lax.axis_size("seq")
    groups = lax.axis_size("dp")
    chans = width // parts
    share = parts // groups
    outer = parts * tiles
    chunk = min(chans, 8)
    size = tiles * chans
    half = width // groups // 2
    scale = 1.0 / math.sqrt(groups * parts * rows)
    first, last, twiddle, fwd, inv = tables(outer)
    place = jnp.stack([lax.axis_index("seq"), lax.axis_index("dp")]).astype(jnp.int32)
    block = jax.ShapeDtypeStruct((parts // 2, size, LANES), F32)
    spectrum = jax.ShapeDtypeStruct((chans * outer, 2 * LANES), F32)
    signal = pltpu.VMEM((width, rows), F32)
    field = pltpu.VMEM((outer * chans, LANES), F32)
    split_rows = pltpu.VMEM((chunk * outer, 2 * LANES), BF16)
    n_blocks = parts // 2 + 1

    inputs = (filter_taps, tok, cot, w_in, w_out)

    def prep_kernel(at_ref, *refs):
        signal_ref, sems = refs[-2:]
        held = refs[-7:-2]
        copies = [
            pltpu.make_async_copy(source, target, sems.at[n])
            for n, (source, target) in enumerate(zip(refs[:5], held))
        ]
        for copy in copies:
            copy.start()
        refs = refs[5:-7]
        copies[0].wait()
        signal_ref[...] = held[0][...].T
        deal(at_ref[0], signal_ref, *refs[:2])
        for copy in copies[1:]:
            copy.wait()
        gate_out, gate_in, values, dmixed = projections(*held[1:])
        signal_ref[...] = values * gate_in
        deal(at_ref[0], signal_ref, *refs[2:4])
        signal_ref[...] = dmixed * gate_out
        deal(at_ref[0], signal_ref, *refs[4:6])

    dealt = call(
        prep_kernel, (place, *inputs), (block,) * 6,
        [pltpu.VMEM(x.shape, x.dtype) for x in inputs] + [signal, pltpu.SemaphoreType.DMA((5,))],
        flops=8 * rows * width * width, space=pltpu.MemorySpace.HBM, grant=PREP_GRANT,
    )
    taps_blocks = exchange(*dealt[:2])
    gated_blocks = exchange(*dealt[2:4])
    dconv_blocks = exchange(*dealt[4:])

    work = chans * outer * LANES * 4 * (3 * 2 * LANES + 6 * outer)

    def split_blocks(refs):
        return refs[0], refs[1], refs[2:n_blocks]

    def loop(step):
        def body(index, carry):
            step(index * chunk, pl.ds(pl.multiple_of(index * chunk * outer, chunk * outer), chunk * outer))
            return carry

        lax.fori_loop(0, chans // chunk, body, 0)

    def taps_spectrum_kernel(at_ref, first_ref, tw_ref, fwd_ref, *refs):
        blocks, (h_ref, x_ref, zh_ref, zl_ref) = split_blocks(refs[:n_blocks]), refs[n_blocks:]
        collect(at_ref[0], x_ref, blocks)

        def step(base, span):
            h_ref[span, :] = forward(x_ref, base, chunk, chans, first_ref, tw_ref, fwd_ref, zh_ref, zl_ref)

        loop(step)

    (taps_spec,) = call(
        taps_spectrum_kernel, (place, first, twiddle, fwd, *taps_blocks), (spectrum,),
        [field, split_rows, split_rows], flops=work,
    )

    def conv_kernel(at_ref, first_ref, last_ref, tw_ref, fwd_ref, inv_ref, h_ref, *refs):
        blocks = split_blocks(refs[:n_blocks])
        g_ref, keep_ref, give_ref, x_ref, y_ref, zh_ref, zl_ref = refs[n_blocks:]
        collect(at_ref[0], x_ref, blocks)

        def step(base, span):
            g = forward(x_ref, base, chunk, chans, first_ref, tw_ref, fwd_ref, zh_ref, zl_ref)
            g_ref[span, :] = g
            product = multiply(halves(h_ref[span, :]), halves(g))
            inverse(product, y_ref, base, chunk, chans, last_ref, tw_ref, inv_ref)

        loop(step)
        deal_field(at_ref[0], y_ref, keep_ref, give_ref)

    gated_spec, conv_keep, conv_give = call(
        conv_kernel, (place, first, last, twiddle, fwd, inv, taps_spec, *gated_blocks),
        (spectrum, block, block), [field, field, split_rows, split_rows], flops=2 * work,
    )
    conv_blocks = exchange(conv_keep, conv_give)
    term = jax.ShapeDtypeStruct((groups, share * size, LANES), F32)

    def corr_kernel(at_ref, first_ref, last_ref, tw_ref, fwd_ref, inv_ref, h_ref, g_ref, *refs):
        blocks = split_blocks(refs[:n_blocks])
        keep_ref, give_ref, term_ref, x_ref, y_ref, k_ref, zh_ref, zl_ref = refs[n_blocks:]
        collect(at_ref[0], x_ref, blocks)

        def step(base, span):
            d = halves(forward(x_ref, base, chunk, chans, first_ref, tw_ref, fwd_ref, zh_ref, zl_ref))
            for spec_ref, field_ref in ((h_ref, y_ref), (g_ref, k_ref)):
                product = correlate(halves(spec_ref[span, :]), d)
                inverse(product, field_ref, base, chunk, chans, last_ref, tw_ref, inv_ref)

        loop(step)
        deal_field(at_ref[0], y_ref, keep_ref, give_ref)
        for k in range(groups):
            for v in range(share):
                dest = at_ref[1] ^ reversed_bits(k, groups)
                row = (dest * share + ((at_ref[0] % share) ^ v)) * size
                term_ref[k, v * size : (v + 1) * size, :] = (
                    k_ref[pl.ds(pl.multiple_of(row, size), size), :] * scale
                )

    dgated_keep, dgated_give, term_parts = call(
        corr_kernel, (place, first, last, twiddle, fwd, inv, taps_spec, gated_spec, *dconv_blocks),
        (block, block, term), [field, field, field, split_rows, split_rows], flops=3 * work,
    )
    dgated_blocks = exchange(dgated_keep, dgated_give)

    def deal_part(at_ref, part_ref, keep_ref, give_ref):
        for k in range(groups):
            for flip, ref in enumerate((keep_ref, give_ref)):
                dest = at_ref[1] ^ reversed_bits(k, groups)
                start = (dest * 2 + ((at_ref[0] & 1) ^ flip)) * half
                ref[k] = part_ref[pl.ds(pl.multiple_of(start, half), half), :]

    def mix_kernel(at_ref, tok_ref, cot_ref, win_ref, wout_ref, skip_ref, *refs):
        blocks = split_blocks(refs[:n_blocks])
        out_ref, dproj_ref, keep_ref, give_ref, c_ref, part_ref = refs[n_blocks:]
        gate_out, gate_in, values, dmixed = projections(tok_ref, cot_ref, win_ref, wout_ref)
        gated = values * gate_in
        collect_signal(at_ref[0], c_ref, blocks)
        conv = c_ref[...] + skip_column(skip_ref, tiles) * gated
        mixed = (conv * gate_out).astype(BF16)
        dproj = (dmixed * conv).astype(BF16)
        dproj_ref[...] = dproj
        out_ref[...] = dot(mixed, wout_ref[...], ((0,), (0,))).astype(BF16)
        part_ref[:, :width] = dot(tok_ref[...], dproj, ((0,), (1,))) * scale
        part_ref[:, width : 2 * width] = dot(mixed, cot_ref[...]) * scale
        product = dmixed * gate_out * gated * scale
        total = product[:, :LANES]
        for t in range(1, tiles):
            total = total + product[:, t * LANES : (t + 1) * LANES]
        part_ref[:, 2 * width :] = total
        deal_part(at_ref, part_ref, keep_ref, give_ref)

    early = 2 * width + LANES
    piece = jax.ShapeDtypeStruct((groups, half, early), F32)
    output, dproj_first, early_keep, early_give = call(
        mix_kernel, (place, tok, cot, w_in, w_out, skip[None, :], *conv_blocks),
        (jax.ShapeDtypeStruct((rows, width), BF16), jax.ShapeDtypeStruct((width, rows), BF16), piece, piece),
        [signal, pltpu.VMEM((width, early), F32)], flops=14 * rows * width * width,
    )
    early_sum = reduce_rows(early_keep, early_give)

    def last_kernel(at_ref, tok_ref, cot_ref, win_ref, wout_ref, skip_ref, dproj_ref, *refs):
        blocks = split_blocks(refs[:n_blocks])
        din_ref, keep_ref, give_ref, c_ref, part_ref = refs[n_blocks:]
        gate_out, gate_in, values, dmixed = projections(tok_ref, cot_ref, win_ref, wout_ref)
        collect_signal(at_ref[0], c_ref, blocks)
        dgated = c_ref[...] + skip_column(skip_ref, tiles) * (dmixed * gate_out)
        dproj = jnp.concatenate([(dgated * values).astype(BF16), (dgated * gate_in).astype(BF16)], axis=0)
        part_ref[...] = dot(tok_ref[...], dproj, ((0,), (1,))) * scale
        deal_part(at_ref, part_ref, keep_ref, give_ref)
        dproj = jnp.concatenate([dproj_ref[...], dproj], axis=0)
        din_ref[...] = dot(dproj, win_ref[...], ((0,), (1,))).astype(BF16)

    piece = jax.ShapeDtypeStruct((groups, half, 2 * width), F32)
    dinput, late_keep, late_give = call(
        last_kernel, (place, tok, cot, w_in, w_out, skip[None, :], dproj_first, *dgated_blocks),
        (jax.ShapeDtypeStruct((rows, width), BF16), piece, piece),
        [signal, pltpu.VMEM((width, 2 * width), F32)], flops=18 * rows * width * width,
    )
    late_sum = reduce_rows(late_keep, late_give)

    grad_sum = spread_rows(jnp.concatenate([early_sum, late_sum], axis=1))
    term_sum = halve(term_parts)
    swap = [
        (i * parts + j, (j // share) * parts + i * share + j % share)
        for i in range(groups)
        for j in range(parts)
    ]
    term_sum = lax.ppermute(term_sum, ("dp", "seq"), swap)
    term_sum = term_sum.reshape(share, size, LANES)
    pieces = [term_sum] + [mirror(term_sum[k], "seq", k) for k in range(1, share)]

    def join_kernel(at_ref, *refs):
        sums, terms = refs[:2], refs[2 : 2 + share]
        in_ref, out_ref, taps_out_ref, skip_out_ref, skip_ref = refs[2 + share :]
        for flip, ref in enumerate(sums):
            row = pl.multiple_of(((at_ref[0] & 1) ^ flip) * half, half)
            span = pl.ds(row, half)
            in_ref[span, :width] = ref[:, :width]
            out_ref[span, :] = ref[:, width : 2 * width]
            skip_ref[span, :] = ref[:, 2 * width : early]
            in_ref[span, width:] = ref[:, early:]
        skip_out_ref[...] = jnp.sum(skip_ref[...], axis=1, keepdims=True).T
        for k in range(share):
            start = pl.multiple_of((k ^ (at_ref[0] % share)) * chans, chans)
            for t in range(tiles):
                span = slice(t * chans, (t + 1) * chans)
                piece = terms[k][span, :] if k else terms[0][0, span, :]
                taps_out_ref[pl.ds(start, chans), t * LANES : (t + 1) * LANES] = piece

    grad_in, grad_out, grad_taps, grad_skip = call(
        join_kernel, (place, *grad_sum, *pieces),
        (
            jax.ShapeDtypeStruct((2 * half, 3 * width), F32),
            jax.ShapeDtypeStruct((2 * half, width), F32),
            jax.ShapeDtypeStruct((share * chans, rows), F32),
            jax.ShapeDtypeStruct((1, 2 * half), F32),
        ),
        [pltpu.VMEM((2 * half, LANES), F32)], flops=rows * width,
    )
    return output[None], dinput[None], grad_in, grad_out, grad_taps.T, grad_skip[0]


def solution(mesh):
    return jax.shard_map(
        shards,
        mesh=mesh,
        in_specs=(P("dp", "seq", None), P("dp", "seq", None), P(), P(), P("seq", None), P()),
        out_specs=(
            P("dp", "seq", None),
            P("dp", "seq", None),
            P("dp", None),
            P("dp", None),
            P("seq", "dp"),
            P("dp"),
        ),
        check_vma=False,
    )
```

```python
import math

import jax
import jax.numpy as jnp
import numpy as np
from jax import lax
from jax.experimental import pallas as pl
from jax.experimental.pallas import tpu as pltpu
from jax.sharding import PartitionSpec as P


LANES = 128
F32 = jnp.float32
BF16 = jnp.bfloat16
SHIFT = 0.25
VMEM_GRANT = 8 * 2**20
PREP_GRANT = 54984704


def split_const(table):
    high = table.astype(BF16)
    low = (table - high.astype(np.float64)).astype(BF16)
    return high, low


def tables(outer):
    length = outer * LANES
    place = np.arange(outer)
    freq = place + SHIFT
    lane = np.arange(LANES)
    angle = 2.0 * np.pi * np.outer(freq, place) / outer
    high, low = split_const(np.concatenate([np.cos(angle), -np.sin(angle)], axis=0))
    first = np.concatenate([high, high, low], axis=1)
    back = np.concatenate([np.cos(angle.T), -np.sin(angle.T)], axis=1) / length
    high, low = split_const(back)
    last = np.concatenate([high, high, low], axis=1)
    turn = 2.0 * np.pi * np.outer(freq, lane) / length
    twiddle = np.stack([np.cos(turn), -np.sin(turn)]).astype(np.float32)
    inner = 2.0 * np.pi * np.outer(lane, lane) / LANES
    cos, sin = np.cos(inner), np.sin(inner)
    fwd = np.stack(split_const(np.block([[cos, -sin], [sin, cos]])))
    inv = np.stack(split_const(np.block([[cos, sin], [-sin, cos]])))
    return [jnp.asarray(t) for t in (first, last, twiddle, fwd, inv)]


def dot(a, b, contract=((1,), (0,))):
    return lax.dot_general(a, b, (contract, ((), ())), preferred_element_type=F32)


def split(x):
    high = x.astype(BF16)
    return high, (x - high.astype(F32)).astype(BF16)


def wide(high, low, ref):
    return dot(high, ref[0]) + dot(low, ref[0]) + dot(high, ref[1])


def multiply(a, b):
    return a[0] * b[0] - a[1] * b[1], a[0] * b[1] + a[1] * b[0]


def correlate(a, b):
    return a[0] * b[0] + a[1] * b[1], a[0] * b[1] - a[1] * b[0]


def halves(x):
    return x[:, :LANES], x[:, LANES:]


def projections(tok_ref, cot_ref, win_ref, wout_ref):
    width = wout_ref.shape[0]
    projected = dot(win_ref[...], tok_ref[...], ((0,), (1,)))
    dmixed = dot(wout_ref[...], cot_ref[...], ((1,), (1,)))
    return projected[:width], projected[width : 2 * width], projected[2 * width :], dmixed


def skip_column(skip_ref, tiles):
    column = jnp.broadcast_to(skip_ref[...], (LANES, skip_ref.shape[1])).T
    return jnp.concatenate([column] * tiles, axis=1)


def deal(me, signal_ref, keep_ref, give_ref):
    count, size, _ = keep_ref.shape
    tiles = signal_ref.shape[1] // LANES
    chans = size // tiles
    for k in range(count):
        for flip, ref in enumerate((keep_ref, give_ref)):
            dest = me ^ (2 * k + flip)
            start = pl.multiple_of(dest * chans, chans)
            for t in range(tiles):
                ref[k, t * chans : (t + 1) * chans, :] = signal_ref[
                    pl.ds(start, chans), t * LANES : (t + 1) * LANES
                ]


def blocks_of(me, keep_ref, got_ref, recv_refs):
    yield me, keep_ref.at[0]
    yield me ^ 1, got_ref.at[0]
    for k, ref in enumerate(recv_refs):
        for flip in range(2):
            yield me ^ (2 * (k + 1) + flip), ref.at[flip]


def collect(me, field_ref, blocks):
    for source, ref in blocks_of(me, *blocks):
        size = ref.shape[0]
        field_ref[pl.ds(pl.multiple_of(source * size, size), size), :] = ref[...]


def collect_signal(me, signal_ref, blocks):
    tiles = signal_ref.shape[1] // LANES
    for source, ref in blocks_of(me, *blocks):
        chans = ref.shape[0] // tiles
        start = pl.multiple_of(source * chans, chans)
        for t in range(tiles):
            signal_ref[pl.ds(start, chans), t * LANES : (t + 1) * LANES] = ref[
                t * chans : (t + 1) * chans, :
            ]


def deal_field(me, field_ref, keep_ref, give_ref):
    count, size, _ = keep_ref.shape
    for k in range(count):
        for flip, ref in enumerate((keep_ref, give_ref)):
            dest = me ^ (2 * k + flip)
            ref[k] = field_ref[pl.ds(pl.multiple_of(dest * size, size), size), :]


def forward(field_ref, base, chunk, chans, first_ref, tw_ref, fwd_ref, zh_ref, zl_ref):
    outer = tw_ref.shape[1]
    tw_re, tw_im = tw_ref[0], tw_ref[1]
    for pair in range(chunk // 2):
        chan = base + 2 * pair
        x = jnp.concatenate(
            [field_ref[pl.ds(chan + side, outer, stride=chans), :] for side in range(2)], axis=1
        )
        high, low = split(x)
        a = dot(first_ref[...], jnp.concatenate([high, low, high], axis=0))
        for side in range(2):
            lanes = slice(side * LANES, (side + 1) * LANES)
            re, im = a[:outer, lanes], a[outer:, lanes]
            z = jnp.concatenate([re * tw_re - im * tw_im, re * tw_im + im * tw_re], axis=1)
            place = slice((2 * pair + side) * outer, (2 * pair + side + 1) * outer)
            zh_ref[place, :], zl_ref[place, :] = split(z)
    return wide(zh_ref[...], zl_ref[...], fwd_ref)


def inverse(pair_of, field_ref, base, chunk, chans, last_ref, tw_ref, inv_ref):
    outer = tw_ref.shape[1]
    tw_re, tw_im = tw_ref[0], tw_ref[1]
    high, low = split(jnp.concatenate(pair_of, axis=1))
    u = wide(high, low, inv_ref)
    for pair in range(chunk // 2):
        sides = []
        for side in range(2):
            start = (2 * pair + side) * outer
            re, im = halves(u[start : start + outer])
            sides.append(jnp.concatenate([re * tw_re + im * tw_im, im * tw_re - re * tw_im], axis=0))
        high, low = split(jnp.concatenate(sides, axis=1))
        y = dot(last_ref[...], jnp.concatenate([high, low, high], axis=0))
        for side in range(2):
            chan = base + 2 * pair + side
            field_ref[pl.ds(chan, outer, stride=chans), :] = y[:, side * LANES : (side + 1) * LANES]


def call(body, operands, outs, scratch=(), flops=0, space=pltpu.VMEM, grant=VMEM_GRANT):
    size = sum(x.size * x.dtype.itemsize for x in list(operands) + list(outs))
    specs = [pl.BlockSpec(memory_space=pltpu.SMEM)]
    specs += [pl.BlockSpec(memory_space=space)] * (len(operands) - 1)
    return pl.pallas_call(
        body,
        out_shape=tuple(outs),
        in_specs=specs,
        out_specs=tuple(pl.BlockSpec(memory_space=pltpu.VMEM) for _ in outs),
        scratch_shapes=list(scratch),
        cost_estimate=pl.CostEstimate(flops=flops, bytes_accessed=size, transcendentals=0),
        compiler_params=pltpu.CompilerParams(vmem_limit_bytes=grant),
    )(*operands)


def mirror(x, axis, mask):
    count = lax.axis_size(axis)
    return lax.ppermute(x, axis, [(i, i ^ mask) for i in range(count)])


def exchange(keep, give):
    got = mirror(give, "seq", 1)
    recv = []
    for k in range(1, keep.shape[0]):
        both = jnp.stack([keep[k], got[k]])
        recv.append(mirror(both, "seq", 2 * k))
    return [keep, got] + recv


def tree_sum(terms):
    while len(terms) > 1:
        terms = [a + b for a, b in zip(terms[::2], terms[1::2])]
    return terms[0]


def reversed_bits(slot, count):
    value = 0
    while count > 1:
        value = 2 * value + slot % 2
        slot //= 2
        count //= 2
    return value


def halve(x):
    mask = 1
    while x.shape[0] > 1:
        middle = x.shape[0] // 2
        x = x[:middle] + mirror(x[middle:], "dp", mask)
        mask *= 2
    return x[0]


def reduce_rows(keep, give):
    return halve(keep + mirror(give, "seq", 1))


def spread_rows(held):
    whole = [held]
    for k in range(1, lax.axis_size("seq") // 2):
        whole.append(mirror(held, "seq", 2 * k))
    whole = tree_sum(whole)
    return whole, mirror(whole, "seq", 1)


def shards(tokens, cotangent, w_in, w_out, filter_taps, skip):
    width = w_out.shape[0]
    tok, cot = tokens[0], cotangent[0]
    rows = tok.shape[0]
    tiles = rows // LANES
    parts = lax.axis_size("seq")
    groups = lax.axis_size("dp")
    chans = width // parts
    share = parts // groups
    outer = parts * tiles
    chunk = min(chans, 32)
    size = tiles * chans
    half = width // groups // 2
    scale = 1.0 / math.sqrt(groups * parts * rows)
    first, last, twiddle, fwd, inv = tables(outer)
    place = jnp.stack([lax.axis_index("seq"), lax.axis_index("dp")]).astype(jnp.int32)
    block = jax.ShapeDtypeStruct((parts // 2, size, LANES), F32)
    spectrum = jax.ShapeDtypeStruct((chans * outer, 2 * LANES), F32)
    signal = pltpu.VMEM((width, rows), F32)
    field = pltpu.VMEM((outer * chans, LANES), F32)
    split_rows = pltpu.VMEM((chunk * outer, 2 * LANES), BF16)
    n_blocks = parts // 2 + 1

    inputs = (filter_taps, tok, cot, w_in, w_out)

    def prep_kernel(at_ref, *refs):
        signal_ref, sems = refs[-2:]
        held = refs[-7:-2]
        copies = [
            pltpu.make_async_copy(source, target, sems.at[n])
            for n, (source, target) in enumerate(zip(refs[:5], held))
        ]
        for copy in copies:
            copy.start()
        refs = refs[5:-7]
        copies[0].wait()
        signal_ref[...] = held[0][...].T
        deal(at_ref[0], signal_ref, *refs[:2])
        for copy in copies[1:]:
            copy.wait()
        gate_out, gate_in, values, dmixed = projections(*held[1:])
        signal_ref[...] = values * gate_in
        deal(at_ref[0], signal_ref, *refs[2:4])
        signal_ref[...] = dmixed * gate_out
        deal(at_ref[0], signal_ref, *refs[4:6])

    dealt = call(
        prep_kernel, (place, *inputs), (block,) * 6,
        [pltpu.VMEM(x.shape, x.dtype) for x in inputs] + [signal, pltpu.SemaphoreType.DMA((5,))],
        flops=8 * rows * width * width, space=pltpu.MemorySpace.HBM, grant=PREP_GRANT,
    )
    taps_blocks = exchange(*dealt[:2])
    gated_blocks = exchange(*dealt[2:4])
    dconv_blocks = exchange(*dealt[4:])

    work = chans * outer * LANES * 4 * (3 * 2 * LANES + 6 * outer)

    def split_blocks(refs):
        return refs[0], refs[1], refs[2:n_blocks]

    def loop(step):
        def body(index, carry):
            step(index * chunk, pl.ds(pl.multiple_of(index * chunk * outer, chunk * outer), chunk * outer))
            return carry

        lax.fori_loop(0, chans // chunk, body, 0)

    def taps_spectrum_kernel(at_ref, first_ref, tw_ref, fwd_ref, *refs):
        blocks, (h_ref, x_ref, zh_ref, zl_ref) = split_blocks(refs[:n_blocks]), refs[n_blocks:]
        collect(at_ref[0], x_ref, blocks)

        def step(base, span):
            h_ref[span, :] = forward(x_ref, base, chunk, chans, first_ref, tw_ref, fwd_ref, zh_ref, zl_ref)

        loop(step)

    (taps_spec,) = call(
        taps_spectrum_kernel, (place, first, twiddle, fwd, *taps_blocks), (spectrum,),
        [field, split_rows, split_rows], flops=work,
    )

    def conv_kernel(at_ref, first_ref, last_ref, tw_ref, fwd_ref, inv_ref, h_ref, *refs):
        blocks = split_blocks(refs[:n_blocks])
        g_ref, keep_ref, give_ref, x_ref, y_ref, zh_ref, zl_ref = refs[n_blocks:]
        collect(at_ref[0], x_ref, blocks)

        def step(base, span):
            g = forward(x_ref, base, chunk, chans, first_ref, tw_ref, fwd_ref, zh_ref, zl_ref)
            g_ref[span, :] = g
            product = multiply(halves(h_ref[span, :]), halves(g))
            inverse(product, y_ref, base, chunk, chans, last_ref, tw_ref, inv_ref)

        loop(step)
        deal_field(at_ref[0], y_ref, keep_ref, give_ref)

    gated_spec, conv_keep, conv_give = call(
        conv_kernel, (place, first, last, twiddle, fwd, inv, taps_spec, *gated_blocks),
        (spectrum, block, block), [field, field, split_rows, split_rows], flops=2 * work,
    )
    conv_blocks = exchange(conv_keep, conv_give)
    term = jax.ShapeDtypeStruct((groups, share * size, LANES), F32)

    def corr_kernel(at_ref, first_ref, last_ref, tw_ref, fwd_ref, inv_ref, h_ref, g_ref, *refs):
        blocks = split_blocks(refs[:n_blocks])
        keep_ref, give_ref, term_ref, x_ref, y_ref, k_ref, zh_ref, zl_ref = refs[n_blocks:]
        collect(at_ref[0], x_ref, blocks)

        def step(base, span):
            d = halves(forward(x_ref, base, chunk, chans, first_ref, tw_ref, fwd_ref, zh_ref, zl_ref))
            for spec_ref, field_ref in ((h_ref, y_ref), (g_ref, k_ref)):
                product = correlate(halves(spec_ref[span, :]), d)
                inverse(product, field_ref, base, chunk, chans, last_ref, tw_ref, inv_ref)

        loop(step)
        deal_field(at_ref[0], y_ref, keep_ref, give_ref)
        for k in range(groups):
            for v in range(share):
                dest = at_ref[1] ^ reversed_bits(k, groups)
                dest = dest ^ (at_ref[0] // share)
                row = (dest * share + ((at_ref[0] % share) ^ v)) * size
                term_ref[k, v * size : (v + 1) * size, :] = (
                    k_ref[pl.ds(pl.multiple_of(row, size), size), :] * scale
                )

    dgated_keep, dgated_give, term_parts = call(
        corr_kernel, (place, first, last, twiddle, fwd, inv, taps_spec, gated_spec, *dconv_blocks),
        (block, block, term), [field, field, field, split_rows, split_rows], flops=3 * work,
    )
    dgated_blocks = exchange(dgated_keep, dgated_give)

    def deal_part(at_ref, part_ref, keep_ref, give_ref):
        for k in range(groups):
            for flip, ref in enumerate((keep_ref, give_ref)):
                dest = at_ref[1] ^ reversed_bits(k, groups)
                start = (dest * 2 + ((at_ref[0] & 1) ^ flip)) * half
                ref[k] = part_ref[pl.ds(pl.multiple_of(start, half), half), :]

    def mix_kernel(at_ref, tok_ref, cot_ref, win_ref, wout_ref, skip_ref, *refs):
        blocks = split_blocks(refs[:n_blocks])
        mixed_ref, dproj_ref, keep_ref, give_ref, c_ref, part_ref = refs[n_blocks:]
        gate_out, gate_in, values, dmixed = projections(tok_ref, cot_ref, win_ref, wout_ref)
        gated = values * gate_in
        collect_signal(at_ref[0], c_ref, blocks)
        conv = c_ref[...] + skip_column(skip_ref, tiles) * gated
        mixed = (conv * gate_out).astype(BF16)
        dproj = (dmixed * conv).astype(BF16)
        dproj_ref[...] = dproj
        mixed_ref[...] = mixed
        part_ref[:, :width] = dot(tok_ref[...], dproj, ((0,), (1,))) * scale
        part_ref[:, width : 2 * width] = dot(mixed, cot_ref[...]) * scale
        product = dmixed * gate_out * gated * scale
        total = product[:, :LANES]
        for t in range(1, tiles):
            total = total + product[:, t * LANES : (t + 1) * LANES]
        part_ref[:, 2 * width :] = total
        deal_part(at_ref, part_ref, keep_ref, give_ref)

    early = 2 * width + LANES
    piece = jax.ShapeDtypeStruct((groups, half, early), F32)
    mixed, dproj_first, early_keep, early_give = call(
        mix_kernel, (place, tok, cot, w_in, w_out, skip[None, :], *conv_blocks),
        (jax.ShapeDtypeStruct((width, rows), BF16),) * 2 + (piece, piece),
        [signal, pltpu.VMEM((width, early), F32)], flops=14 * rows * width * width,
    )
    early_sum = reduce_rows(early_keep, early_give)

    def last_kernel(at_ref, tok_ref, cot_ref, win_ref, wout_ref, skip_ref, *refs):
        blocks = split_blocks(refs[:n_blocks])
        dproj_late_ref, keep_ref, give_ref, c_ref, part_ref = refs[n_blocks:]
        gate_out, gate_in, values, dmixed = projections(tok_ref, cot_ref, win_ref, wout_ref)
        collect_signal(at_ref[0], c_ref, blocks)
        dgated = c_ref[...] + skip_column(skip_ref, tiles) * (dmixed * gate_out)
        dproj = jnp.concatenate([(dgated * values).astype(BF16), (dgated * gate_in).astype(BF16)], axis=0)
        part_ref[...] = dot(tok_ref[...], dproj, ((0,), (1,))) * scale
        deal_part(at_ref, part_ref, keep_ref, give_ref)
        dproj_late_ref[...] = dproj

    piece = jax.ShapeDtypeStruct((groups, half, 2 * width), F32)
    dproj_late, late_keep, late_give = call(
        last_kernel, (place, tok, cot, w_in, w_out, skip[None, :], *dgated_blocks),
        (jax.ShapeDtypeStruct((2 * width, rows), BF16), piece, piece),
        [signal, pltpu.VMEM((width, 2 * width), F32)], flops=18 * rows * width * width,
    )

    def inputs_kernel(at_ref, win_ref, first_dproj_ref, late_dproj_ref, din_ref):
        dproj = jnp.concatenate([first_dproj_ref[...], late_dproj_ref[...]], axis=0)
        din_ref[...] = dot(dproj, win_ref[...], ((0,), (1,))).astype(BF16)

    (dinput,) = call(
        inputs_kernel, (place, w_in, dproj_first, dproj_late), (jax.ShapeDtypeStruct((rows, width), BF16),),
        flops=6 * rows * width * width,
    )

    def outputs_kernel(at_ref, wout_ref, mixed_ref, out_ref):
        out_ref[...] = dot(mixed_ref[...], wout_ref[...], ((0,), (0,))).astype(BF16)

    (output,) = call(
        outputs_kernel, (place, w_out, mixed), (jax.ShapeDtypeStruct((rows, width), BF16),),
        flops=2 * rows * width * width,
    )
    late_sum = reduce_rows(late_keep, late_give)

    grad_sum = spread_rows(jnp.concatenate([early_sum, late_sum], axis=1))
    term_sum = halve(term_parts)
    swap = [
        (i * parts + j, (j // share) * parts + (i ^ (j // share)) * share + j % share)
        for i in range(groups)
        for j in range(parts)
    ]
    term_sum = lax.ppermute(term_sum, ("dp", "seq"), swap)
    term_sum = term_sum.reshape(share, size, LANES)
    pieces = [term_sum] + [mirror(term_sum[k], "seq", k) for k in range(1, share)]

    def join_kernel(at_ref, *refs):
        sums, terms = refs[:2], refs[2 : 2 + share]
        in_ref, out_ref, taps_out_ref, skip_out_ref, skip_ref = refs[2 + share :]
        for flip, ref in enumerate(sums):
            row = pl.multiple_of(((at_ref[0] & 1) ^ flip) * half, half)
            span = pl.ds(row, half)
            in_ref[span, :width] = ref[:, :width]
            out_ref[span, :] = ref[:, width : 2 * width]
            skip_ref[span, :] = ref[:, 2 * width : early]
            in_ref[span, width:] = ref[:, early:]
        skip_out_ref[...] = jnp.sum(skip_ref[...], axis=1, keepdims=True).T
        for k in range(share):
            start = pl.multiple_of((k ^ (at_ref[0] % share)) * chans, chans)
            for t in range(tiles):
                span = slice(t * chans, (t + 1) * chans)
                piece = terms[k][span, :] if k else terms[0][0, span, :]
                taps_out_ref[pl.ds(start, chans), t * LANES : (t + 1) * LANES] = piece

    grad_in, grad_out, grad_taps, grad_skip = call(
        join_kernel, (place, *grad_sum, *pieces),
        (
            jax.ShapeDtypeStruct((2 * half, 3 * width), F32),
            jax.ShapeDtypeStruct((2 * half, width), F32),
            jax.ShapeDtypeStruct((share * chans, rows), F32),
            jax.ShapeDtypeStruct((1, 2 * half), F32),
        ),
        [pltpu.VMEM((2 * half, LANES), F32)], flops=rows * width,
    )
    return output[None], dinput[None], grad_in, grad_out, grad_taps.T, grad_skip[0]


def solution(mesh):
    return jax.shard_map(
        shards,
        mesh=mesh,
        in_specs=(P("dp", "seq", None), P("dp", "seq", None), P(), P(), P("seq", None), P()),
        out_specs=(
            P("dp", "seq", None),
            P("dp", "seq", None),
            P("dp", None),
            P("dp", None),
            P("seq", "dp"),
            P("dp"),
        ),
        check_vma=False,
    )
```

```python
import math

import jax
import jax.numpy as jnp
import numpy as np
from jax import lax
from jax.experimental import pallas as pl
from jax.experimental.pallas import tpu as pltpu
from jax.sharding import PartitionSpec as P


LANES = 128
F32 = jnp.float32
BF16 = jnp.bfloat16
SHIFT = 0.25
VMEM_GRANT = 8 * 2**20


def split_const(table):
    high = table.astype(BF16)
    low = (table - high.astype(np.float64)).astype(BF16)
    return high, low


def tables(outer):
    length = outer * LANES
    place = np.arange(outer)
    freq = place + SHIFT
    lane = np.arange(LANES)
    angle = 2.0 * np.pi * np.outer(freq, place) / outer
    high, low = split_const(np.concatenate([np.cos(angle), -np.sin(angle)], axis=0))
    first = np.concatenate([high, high, low], axis=1)
    back = np.concatenate([np.cos(angle.T), -np.sin(angle.T)], axis=1) / length
    high, low = split_const(back)
    last = np.concatenate([high, high, low], axis=1)
    turn = 2.0 * np.pi * np.outer(freq, lane) / length
    twiddle = np.stack([np.cos(turn), -np.sin(turn)]).astype(np.float32)
    inner = 2.0 * np.pi * np.outer(lane, lane) / LANES
    cos, sin = np.cos(inner), np.sin(inner)
    fwd = np.stack(split_const(np.block([[cos, -sin], [sin, cos]])))
    inv = np.stack(split_const(np.block([[cos, sin], [-sin, cos]])))
    return [jnp.asarray(t) for t in (first, last, twiddle, fwd, inv)]


def dot(a, b, contract=((1,), (0,))):
    return lax.dot_general(a, b, (contract, ((), ())), preferred_element_type=F32)


def split(x):
    high = x.astype(BF16)
    return high, (x - high.astype(F32)).astype(BF16)


def wide(high, low, ref):
    return dot(high, ref[0]) + dot(low, ref[0]) + dot(high, ref[1])


def multiply(a, b):
    return a[0] * b[0] - a[1] * b[1], a[0] * b[1] + a[1] * b[0]


def correlate(a, b):
    return a[0] * b[0] + a[1] * b[1], a[0] * b[1] - a[1] * b[0]


def halves(x):
    return x[:, :LANES], x[:, LANES:]


def projections(tok_ref, cot_ref, win_ref, wout_ref):
    width = wout_ref.shape[0]
    projected = dot(win_ref[...], tok_ref[...], ((0,), (1,)))
    dmixed = dot(wout_ref[...], cot_ref[...], ((1,), (1,)))
    return projected[:width], projected[width : 2 * width], projected[2 * width :], dmixed


def skip_column(skip_ref, tiles):
    column = jnp.broadcast_to(skip_ref[...], (LANES, skip_ref.shape[1])).T
    return jnp.concatenate([column] * tiles, axis=1)


def deal(me, signal_ref, keep_ref, give_ref):
    count, size, _ = keep_ref.shape
    tiles = signal_ref.shape[1] // LANES
    chans = size // tiles
    for k in range(count):
        for flip, ref in enumerate((keep_ref, give_ref)):
            dest = me ^ (2 * k + flip)
            start = pl.multiple_of(dest * chans, chans)
            for t in range(tiles):
                ref[k, t * chans : (t + 1) * chans, :] = signal_ref[
                    pl.ds(start, chans), t * LANES : (t + 1) * LANES
                ]


def blocks_of(me, keep_ref, got_ref, recv_refs):
    yield me, keep_ref.at[0]
    yield me ^ 1, got_ref.at[0]
    for k, ref in enumerate(recv_refs):
        for flip in range(2):
            yield me ^ (2 * (k + 1) + flip), ref.at[flip]


def collect(me, field_ref, blocks):
    for source, ref in blocks_of(me, *blocks):
        size = ref.shape[0]
        field_ref[pl.ds(pl.multiple_of(source * size, size), size), :] = ref[...]


def collect_signal(me, signal_ref, blocks):
    tiles = signal_ref.shape[1] // LANES
    for source, ref in blocks_of(me, *blocks):
        chans = ref.shape[0] // tiles
        start = pl.multiple_of(source * chans, chans)
        for t in range(tiles):
            signal_ref[pl.ds(start, chans), t * LANES : (t + 1) * LANES] = ref[
                t * chans : (t + 1) * chans, :
            ]


def deal_field(me, field_ref, keep_ref, give_ref):
    count, size, _ = keep_ref.shape
    for k in range(count):
        for flip, ref in enumerate((keep_ref, give_ref)):
            dest = me ^ (2 * k + flip)
            ref[k] = field_ref[pl.ds(pl.multiple_of(dest * size, size), size), :]


def forward(field_ref, base, chunk, chans, first_ref, tw_ref, fwd_ref, zh_ref, zl_ref):
    outer = tw_ref.shape[1]
    tw_re, tw_im = tw_ref[0], tw_ref[1]
    for pair in range(chunk // 2):
        chan = base + 2 * pair
        x = jnp.concatenate(
            [field_ref[pl.ds(chan + side, outer, stride=chans), :] for side in range(2)], axis=1
        )
        high, low = split(x)
        a = dot(first_ref[...], jnp.concatenate([high, low, high], axis=0))
        for side in range(2):
            lanes = slice(side * LANES, (side + 1) * LANES)
            re, im = a[:outer, lanes], a[outer:, lanes]
            z = jnp.concatenate([re * tw_re - im * tw_im, re * tw_im + im * tw_re], axis=1)
            place = slice((2 * pair + side) * outer, (2 * pair + side + 1) * outer)
            zh_ref[place, :], zl_ref[place, :] = split(z)
    return wide(zh_ref[...], zl_ref[...], fwd_ref)


def inverse(pair_of, field_ref, base, chunk, chans, last_ref, tw_ref, inv_ref):
    outer = tw_ref.shape[1]
    tw_re, tw_im = tw_ref[0], tw_ref[1]
    high, low = split(jnp.concatenate(pair_of, axis=1))
    u = wide(high, low, inv_ref)
    for pair in range(chunk // 2):
        sides = []
        for side in range(2):
            start = (2 * pair + side) * outer
            re, im = halves(u[start : start + outer])
            sides.append(jnp.concatenate([re * tw_re + im * tw_im, im * tw_re - re * tw_im], axis=0))
        high, low = split(jnp.concatenate(sides, axis=1))
        y = dot(last_ref[...], jnp.concatenate([high, low, high], axis=0))
        for side in range(2):
            chan = base + 2 * pair + side
            field_ref[pl.ds(chan, outer, stride=chans), :] = y[:, side * LANES : (side + 1) * LANES]


def call(body, operands, outs, scratch=(), flops=0):
    size = sum(x.size * x.dtype.itemsize for x in list(operands) + list(outs))
    specs = [pl.BlockSpec(memory_space=pltpu.SMEM)]
    specs += [pl.BlockSpec(memory_space=pltpu.VMEM)] * (len(operands) - 1)
    return pl.pallas_call(
        body,
        out_shape=tuple(outs),
        in_specs=specs,
        out_specs=tuple(pl.BlockSpec(memory_space=pltpu.VMEM) for _ in outs),
        scratch_shapes=list(scratch),
        cost_estimate=pl.CostEstimate(flops=flops, bytes_accessed=size, transcendentals=0),
        compiler_params=pltpu.CompilerParams(vmem_limit_bytes=VMEM_GRANT),
    )(*operands)


def mirror(x, axis, mask):
    count = lax.axis_size(axis)
    return lax.ppermute(x, axis, [(i, i ^ mask) for i in range(count)])


def exchange(keep, give):
    got = mirror(give, "seq", 1)
    recv = []
    for k in range(1, keep.shape[0]):
        both = jnp.stack([keep[k], got[k]])
        recv.append(mirror(both, "seq", 2 * k))
    return [keep, got] + recv


def tree_sum(terms):
    while len(terms) > 1:
        terms = [a + b for a, b in zip(terms[::2], terms[1::2])]
    return terms[0]


def reversed_bits(slot, count):
    value = 0
    while count > 1:
        value = 2 * value + slot % 2
        slot //= 2
        count //= 2
    return value


def halve(x):
    mask = 1
    while x.shape[0] > 1:
        middle = x.shape[0] // 2
        x = x[:middle] + mirror(x[middle:], "dp", mask)
        mask *= 2
    return x[0]


def reduce_rows(keep, give):
    return halve(keep + mirror(give, "seq", 1))


def spread_rows(held):
    whole = [held]
    for k in range(1, lax.axis_size("seq") // 2):
        whole.append(mirror(held, "seq", 2 * k))
    whole = tree_sum(whole)
    return whole, mirror(whole, "seq", 1)


def shards(tokens, cotangent, w_in, w_out, filter_taps, skip):
    width = w_out.shape[0]
    tok, cot = tokens[0], cotangent[0]
    rows = tok.shape[0]
    tiles = rows // LANES
    parts = lax.axis_size("seq")
    groups = lax.axis_size("dp")
    chans = width // parts
    share = parts // groups
    outer = parts * tiles
    chunk = min(chans, 32)
    size = tiles * chans
    half = width // groups // 2
    scale = 1.0 / math.sqrt(groups * parts * rows)
    first, last, twiddle, fwd, inv = tables(outer)
    place = jnp.stack([lax.axis_index("seq"), lax.axis_index("dp")]).astype(jnp.int32)
    block = jax.ShapeDtypeStruct((parts // 2, size, LANES), F32)
    spectrum = jax.ShapeDtypeStruct((chans * outer, 2 * LANES), F32)
    signal = pltpu.VMEM((width, rows), F32)
    field = pltpu.VMEM((outer * chans, LANES), F32)
    split_rows = pltpu.VMEM((chunk * outer, 2 * LANES), BF16)
    n_blocks = parts // 2 + 1

    def taps_kernel(at_ref, taps_ref, keep_ref, give_ref, signal_ref):
        signal_ref[...] = taps_ref[...].T
        deal(at_ref[0], signal_ref, keep_ref, give_ref)

    taps_blocks = exchange(*call(taps_kernel, (place, filter_taps), (block, block), [signal]))

    def prep_kernel(at_ref, tok_ref, cot_ref, win_ref, wout_ref, *refs):
        signal_ref = refs[-1]
        gate_out, gate_in, values, dmixed = projections(tok_ref, cot_ref, win_ref, wout_ref)
        signal_ref[...] = values * gate_in
        deal(at_ref[0], signal_ref, *refs[:2])
        signal_ref[...] = dmixed * gate_out
        deal(at_ref[0], signal_ref, *refs[2:4])

    dealt = call(
        prep_kernel, (place, tok, cot, w_in, w_out), (block,) * 4, [signal],
        flops=8 * rows * width * width,
    )
    gated_blocks = exchange(*dealt[:2])
    dconv_blocks = exchange(*dealt[2:])

    work = chans * outer * LANES * 4 * (3 * 2 * LANES + 6 * outer)

    def split_blocks(refs):
        return refs[0], refs[1], refs[2:n_blocks]

    def loop(step):
        def body(index, carry):
            step(index * chunk, pl.ds(pl.multiple_of(index * chunk * outer, chunk * outer), chunk * outer))
            return carry

        lax.fori_loop(0, chans // chunk, body, 0)

    def taps_spectrum_kernel(at_ref, first_ref, tw_ref, fwd_ref, *refs):
        blocks, (h_ref, x_ref, zh_ref, zl_ref) = split_blocks(refs[:n_blocks]), refs[n_blocks:]
        collect(at_ref[0], x_ref, blocks)

        def step(base, span):
            h_ref[span, :] = forward(x_ref, base, chunk, chans, first_ref, tw_ref, fwd_ref, zh_ref, zl_ref)

        loop(step)

    (taps_spec,) = call(
        taps_spectrum_kernel, (place, first, twiddle, fwd, *taps_blocks), (spectrum,),
        [field, split_rows, split_rows], flops=work,
    )

    def conv_kernel(at_ref, first_ref, last_ref, tw_ref, fwd_ref, inv_ref, h_ref, *refs):
        blocks = split_blocks(refs[:n_blocks])
        g_ref, keep_ref, give_ref, x_ref, y_ref, zh_ref, zl_ref = refs[n_blocks:]
        collect(at_ref[0], x_ref, blocks)

        def step(base, span):
            g = forward(x_ref, base, chunk, chans, first_ref, tw_ref, fwd_ref, zh_ref, zl_ref)
            g_ref[span, :] = g
            product = multiply(halves(h_ref[span, :]), halves(g))
            inverse(product, y_ref, base, chunk, chans, last_ref, tw_ref, inv_ref)

        loop(step)
        deal_field(at_ref[0], y_ref, keep_ref, give_ref)

    gated_spec, conv_keep, conv_give = call(
        conv_kernel, (place, first, last, twiddle, fwd, inv, taps_spec, *gated_blocks),
        (spectrum, block, block), [field, field, split_rows, split_rows], flops=2 * work,
    )
    conv_blocks = exchange(conv_keep, conv_give)
    term = jax.ShapeDtypeStruct((groups, share * size, LANES), F32)

    def corr_kernel(at_ref, first_ref, last_ref, tw_ref, fwd_ref, inv_ref, h_ref, g_ref, *refs):
        blocks = split_blocks(refs[:n_blocks])
        keep_ref, give_ref, term_ref, x_ref, y_ref, k_ref, zh_ref, zl_ref = refs[n_blocks:]
        collect(at_ref[0], x_ref, blocks)

        def step(base, span):
            d = halves(forward(x_ref, base, chunk, chans, first_ref, tw_ref, fwd_ref, zh_ref, zl_ref))
            for spec_ref, field_ref in ((h_ref, y_ref), (g_ref, k_ref)):
                product = correlate(halves(spec_ref[span, :]), d)
                inverse(product, field_ref, base, chunk, chans, last_ref, tw_ref, inv_ref)

        loop(step)
        deal_field(at_ref[0], y_ref, keep_ref, give_ref)
        for k in range(groups):
            for v in range(share):
                dest = at_ref[1] ^ reversed_bits(k, groups)
                dest = dest ^ (at_ref[0] // share)
                row = (dest * share + ((at_ref[0] % share) ^ v)) * size
                term_ref[k, v * size : (v + 1) * size, :] = (
                    k_ref[pl.ds(pl.multiple_of(row, size), size), :] * scale
                )

    dgated_keep, dgated_give, term_parts = call(
        corr_kernel, (place, first, last, twiddle, fwd, inv, taps_spec, gated_spec, *dconv_blocks),
        (block, block, term), [field, field, field, split_rows, split_rows], flops=3 * work,
    )
    dgated_blocks = exchange(dgated_keep, dgated_give)

    def deal_part(at_ref, part_ref, keep_ref, give_ref):
        for k in range(groups):
            for flip, ref in enumerate((keep_ref, give_ref)):
                dest = at_ref[1] ^ reversed_bits(k, groups)
                start = (dest * 2 + ((at_ref[0] & 1) ^ flip)) * half
                ref[k] = part_ref[pl.ds(pl.multiple_of(start, half), half), :]

    def mix_kernel(at_ref, tok_ref, cot_ref, win_ref, wout_ref, skip_ref, *refs):
        blocks = split_blocks(refs[:n_blocks])
        mixed_ref, dproj_ref, keep_ref, give_ref, c_ref, part_ref = refs[n_blocks:]
        gate_out, gate_in, values, dmixed = projections(tok_ref, cot_ref, win_ref, wout_ref)
        gated = values * gate_in
        collect_signal(at_ref[0], c_ref, blocks)
        conv = c_ref[...] + skip_column(skip_ref, tiles) * gated
        mixed = (conv * gate_out).astype(BF16)
        dproj = (dmixed * conv).astype(BF16)
        dproj_ref[...] = dproj
        mixed_ref[...] = mixed
        part_ref[:, :width] = dot(tok_ref[...], dproj, ((0,), (1,))) * scale
        part_ref[:, width : 2 * width] = dot(mixed, cot_ref[...]) * scale
        product = dmixed * gate_out * gated * scale
        total = product[:, :LANES]
        for t in range(1, tiles):
            total = total + product[:, t * LANES : (t + 1) * LANES]
        part_ref[:, 2 * width :] = total
        deal_part(at_ref, part_ref, keep_ref, give_ref)

    early = 2 * width + LANES
    piece = jax.ShapeDtypeStruct((groups, half, early), F32)
    mixed, dproj_first, early_keep, early_give = call(
        mix_kernel, (place, tok, cot, w_in, w_out, skip[None, :], *conv_blocks),
        (jax.ShapeDtypeStruct((width, rows), BF16),) * 2 + (piece, piece),
        [signal, pltpu.VMEM((width, early), F32)], flops=14 * rows * width * width,
    )
    early_sum = reduce_rows(early_keep, early_give)

    def last_kernel(at_ref, tok_ref, cot_ref, win_ref, wout_ref, skip_ref, *refs):
        blocks = split_blocks(refs[:n_blocks])
        dproj_late_ref, keep_ref, give_ref, c_ref, part_ref = refs[n_blocks:]
        gate_out, gate_in, values, dmixed = projections(tok_ref, cot_ref, win_ref, wout_ref)
        collect_signal(at_ref[0], c_ref, blocks)
        dgated = c_ref[...] + skip_column(skip_ref, tiles) * (dmixed * gate_out)
        dproj = jnp.concatenate([(dgated * values).astype(BF16), (dgated * gate_in).astype(BF16)], axis=0)
        part_ref[...] = dot(tok_ref[...], dproj, ((0,), (1,))) * scale
        deal_part(at_ref, part_ref, keep_ref, give_ref)
        dproj_late_ref[...] = dproj

    piece = jax.ShapeDtypeStruct((groups, half, 2 * width), F32)
    dproj_late, late_keep, late_give = call(
        last_kernel, (place, tok, cot, w_in, w_out, skip[None, :], *dgated_blocks),
        (jax.ShapeDtypeStruct((2 * width, rows), BF16), piece, piece),
        [signal, pltpu.VMEM((width, 2 * width), F32)], flops=18 * rows * width * width,
    )

    def inputs_kernel(at_ref, win_ref, first_dproj_ref, late_dproj_ref, din_ref):
        dproj = jnp.concatenate([first_dproj_ref[...], late_dproj_ref[...]], axis=0)
        din_ref[...] = dot(dproj, win_ref[...], ((0,), (1,))).astype(BF16)

    (dinput,) = call(
        inputs_kernel, (place, w_in, dproj_first, dproj_late), (jax.ShapeDtypeStruct((rows, width), BF16),),
        flops=6 * rows * width * width,
    )

    def outputs_kernel(at_ref, wout_ref, mixed_ref, out_ref):
        out_ref[...] = dot(mixed_ref[...], wout_ref[...], ((0,), (0,))).astype(BF16)

    (output,) = call(
        outputs_kernel, (place, w_out, mixed), (jax.ShapeDtypeStruct((rows, width), BF16),),
        flops=2 * rows * width * width,
    )
    late_sum = reduce_rows(late_keep, late_give)

    grad_sum = spread_rows(jnp.concatenate([early_sum, late_sum], axis=1))
    term_sum = halve(term_parts)
    swap = [
        (i * parts + j, (j // share) * parts + (i ^ (j // share)) * share + j % share)
        for i in range(groups)
        for j in range(parts)
    ]
    term_sum = lax.ppermute(term_sum, ("dp", "seq"), swap)
    term_sum = term_sum.reshape(share, size, LANES)
    pieces = [term_sum] + [mirror(term_sum[k], "seq", k) for k in range(1, share)]

    def join_kernel(at_ref, *refs):
        sums, terms = refs[:2], refs[2 : 2 + share]
        in_ref, out_ref, taps_out_ref, skip_out_ref, skip_ref = refs[2 + share :]
        for flip, ref in enumerate(sums):
            row = pl.multiple_of(((at_ref[0] & 1) ^ flip) * half, half)
            span = pl.ds(row, half)
            in_ref[span, :width] = ref[:, :width]
            out_ref[span, :] = ref[:, width : 2 * width]
            skip_ref[span, :] = ref[:, 2 * width : early]
            in_ref[span, width:] = ref[:, early:]
        skip_out_ref[...] = jnp.sum(skip_ref[...], axis=1, keepdims=True).T
        for k in range(share):
            start = pl.multiple_of((k ^ (at_ref[0] % share)) * chans, chans)
            for t in range(tiles):
                span = slice(t * chans, (t + 1) * chans)
                piece = terms[k][span, :] if k else terms[0][0, span, :]
                taps_out_ref[pl.ds(start, chans), t * LANES : (t + 1) * LANES] = piece

    grad_in, grad_out, grad_taps, grad_skip = call(
        join_kernel, (place, *grad_sum, *pieces),
        (
            jax.ShapeDtypeStruct((2 * half, 3 * width), F32),
            jax.ShapeDtypeStruct((2 * half, width), F32),
            jax.ShapeDtypeStruct((share * chans, rows), F32),
            jax.ShapeDtypeStruct((1, 2 * half), F32),
        ),
        [pltpu.VMEM((2 * half, LANES), F32)], flops=rows * width,
    )
    return output[None], dinput[None], grad_in, grad_out, grad_taps.T, grad_skip[0]


def solution(mesh):
    return jax.shard_map(
        shards,
        mesh=mesh,
        in_specs=(P("dp", "seq", None), P("dp", "seq", None), P(), P(), P("seq", None), P()),
        out_specs=(
            P("dp", "seq", None),
            P("dp", "seq", None),
            P("dp", None),
            P("dp", None),
            P("seq", "dp"),
            P("dp"),
        ),
        check_vma=False,
    )
```

```python
import math

import jax
import jax.numpy as jnp
import numpy as np
from jax import lax
from jax.experimental import pallas as pl
from jax.experimental.pallas import tpu as pltpu
from jax.sharding import PartitionSpec as P


LANES = 128
F32 = jnp.float32
BF16 = jnp.bfloat16
SHIFT = 0.25
VMEM_GRANT = 8 * 2**20


def split_const(table):
    high = table.astype(BF16)
    low = (table - high.astype(np.float64)).astype(BF16)
    return high, low


def tables(outer):
    length = outer * LANES
    place = np.arange(outer)
    freq = place + SHIFT
    lane = np.arange(LANES)
    angle = 2.0 * np.pi * np.outer(freq, place) / outer
    high, low = split_const(np.concatenate([np.cos(angle), -np.sin(angle)], axis=0))
    first = np.concatenate([high, high, low], axis=1)
    back = np.concatenate([np.cos(angle.T), -np.sin(angle.T)], axis=1) / length
    high, low = split_const(back)
    last = np.concatenate([high, high, low], axis=1)
    turn = 2.0 * np.pi * np.outer(freq, lane) / length
    twiddle = np.stack([np.cos(turn), -np.sin(turn)]).astype(np.float32)
    inner = 2.0 * np.pi * np.outer(lane, lane) / LANES
    cos, sin = np.cos(inner), np.sin(inner)
    fwd = np.stack(split_const(np.block([[cos, -sin], [sin, cos]])))
    inv = np.stack(split_const(np.block([[cos, sin], [-sin, cos]])))
    return [jnp.asarray(t) for t in (first, last, twiddle, fwd, inv)]


def dot(a, b, contract=((1,), (0,))):
    return lax.dot_general(a, b, (contract, ((), ())), preferred_element_type=F32)


def split(x):
    high = x.astype(BF16)
    return high, (x - high.astype(F32)).astype(BF16)


def wide(high, low, ref):
    return dot(high, ref[0]) + dot(low, ref[0]) + dot(high, ref[1])


def multiply(a, b):
    return a[0] * b[0] - a[1] * b[1], a[0] * b[1] + a[1] * b[0]


def correlate(a, b):
    return a[0] * b[0] + a[1] * b[1], a[0] * b[1] - a[1] * b[0]


def halves(x):
    return x[:, :LANES], x[:, LANES:]


def projections(tok_ref, cot_ref, win_ref, wout_ref):
    width = wout_ref.shape[0]
    projected = dot(win_ref[...], tok_ref[...], ((0,), (1,)))
    dmixed = dot(wout_ref[...], cot_ref[...], ((1,), (1,)))
    return projected[:width], projected[width : 2 * width], projected[2 * width :], dmixed


def skip_column(skip_ref, tiles):
    column = jnp.broadcast_to(skip_ref[...], (LANES, skip_ref.shape[1])).T
    return jnp.concatenate([column] * tiles, axis=1)


def deal(me, signal_ref, keep_ref, give_ref):
    count, size, _ = keep_ref.shape
    tiles = signal_ref.shape[1] // LANES
    chans = size // tiles
    for k in range(count):
        for flip, ref in enumerate((keep_ref, give_ref)):
            dest = me ^ (2 * k + flip)
            start = pl.multiple_of(dest * chans, chans)
            for t in range(tiles):
                ref[k, t * chans : (t + 1) * chans, :] = signal_ref[
                    pl.ds(start, chans), t * LANES : (t + 1) * LANES
                ]


def blocks_of(me, keep_ref, got_ref, recv_refs):
    yield me, keep_ref.at[0]
    yield me ^ 1, got_ref.at[0]
    for k, ref in enumerate(recv_refs):
        for flip in range(2):
            yield me ^ (2 * (k + 1) + flip), ref.at[flip]


def collect(me, field_ref, blocks):
    for source, ref in blocks_of(me, *blocks):
        size = ref.shape[0]
        field_ref[pl.ds(pl.multiple_of(source * size, size), size), :] = ref[...]


def collect_signal(me, signal_ref, blocks):
    tiles = signal_ref.shape[1] // LANES
    for source, ref in blocks_of(me, *blocks):
        chans = ref.shape[0] // tiles
        start = pl.multiple_of(source * chans, chans)
        for t in range(tiles):
            signal_ref[pl.ds(start, chans), t * LANES : (t + 1) * LANES] = ref[
                t * chans : (t + 1) * chans, :
            ]


def deal_field(me, field_ref, keep_ref, give_ref):
    count, size, _ = keep_ref.shape
    for k in range(count):
        for flip, ref in enumerate((keep_ref, give_ref)):
            dest = me ^ (2 * k + flip)
            ref[k] = field_ref[pl.ds(pl.multiple_of(dest * size, size), size), :]


def forward(field_ref, base, chunk, chans, first_ref, tw_ref, fwd_ref, zh_ref, zl_ref):
    outer = tw_ref.shape[1]
    tw_re, tw_im = tw_ref[0], tw_ref[1]
    for pair in range(chunk // 2):
        chan = base + 2 * pair
        x = jnp.concatenate(
            [field_ref[pl.ds(chan + side, outer, stride=chans), :] for side in range(2)], axis=1
        )
        high, low = split(x)
        a = dot(first_ref[...], jnp.concatenate([high, low, high], axis=0))
        for side in range(2):
            lanes = slice(side * LANES, (side + 1) * LANES)
            re, im = a[:outer, lanes], a[outer:, lanes]
            z = jnp.concatenate([re * tw_re - im * tw_im, re * tw_im + im * tw_re], axis=1)
            place = slice((2 * pair + side) * outer, (2 * pair + side + 1) * outer)
            zh_ref[place, :], zl_ref[place, :] = split(z)
    return wide(zh_ref[...], zl_ref[...], fwd_ref)


def inverse(pair_of, field_ref, base, chunk, chans, last_ref, tw_ref, inv_ref):
    outer = tw_ref.shape[1]
    tw_re, tw_im = tw_ref[0], tw_ref[1]
    high, low = split(jnp.concatenate(pair_of, axis=1))
    u = wide(high, low, inv_ref)
    for pair in range(chunk // 2):
        sides = []
        for side in range(2):
            start = (2 * pair + side) * outer
            re, im = halves(u[start : start + outer])
            sides.append(jnp.concatenate([re * tw_re + im * tw_im, im * tw_re - re * tw_im], axis=0))
        high, low = split(jnp.concatenate(sides, axis=1))
        y = dot(last_ref[...], jnp.concatenate([high, low, high], axis=0))
        for side in range(2):
            chan = base + 2 * pair + side
            field_ref[pl.ds(chan, outer, stride=chans), :] = y[:, side * LANES : (side + 1) * LANES]


def call(body, operands, outs, scratch=(), flops=0):
    operands = operands[1:]
    specs = [pl.BlockSpec(memory_space=pltpu.VMEM)] * len(operands)

    size = sum(x.size * x.dtype.itemsize for x in list(operands) + list(outs))

    def placed(*refs):
        body((lax.axis_index("seq"), lax.axis_index("dp")), *refs)

    return pl.pallas_call(
        placed,
        out_shape=tuple(outs),
        in_specs=specs,
        out_specs=tuple(pl.BlockSpec(memory_space=pltpu.VMEM) for _ in outs),
        scratch_shapes=list(scratch),
        cost_estimate=pl.CostEstimate(flops=flops, bytes_accessed=size, transcendentals=0),
        compiler_params=pltpu.CompilerParams(vmem_limit_bytes=VMEM_GRANT),
    )(*operands)


def mirror(x, axis, mask):
    count = lax.axis_size(axis)
    return lax.ppermute(x, axis, [(i, i ^ mask) for i in range(count)])


def exchange(keep, give):
    got = mirror(give, "seq", 1)
    recv = []
    for k in range(1, keep.shape[0]):
        both = jnp.stack([keep[k], got[k]])
        recv.append(mirror(both, "seq", 2 * k))
    return [keep, got] + recv


def tree_sum(terms):
    while len(terms) > 1:
        terms = [a + b for a, b in zip(terms[::2], terms[1::2])]
    return terms[0]


def reversed_bits(slot, count):
    value = 0
    while count > 1:
        value = 2 * value + slot % 2
        slot //= 2
        count //= 2
    return value


def halve(x):
    mask = 1
    while x.shape[0] > 1:
        middle = x.shape[0] // 2
        x = x[:middle] + mirror(x[middle:], "dp", mask)
        mask *= 2
    return x[0]


def reduce_rows(keep, give):
    return halve(keep + mirror(give, "seq", 1))


def spread_rows(held):
    whole = [held]
    for k in range(1, lax.axis_size("seq") // 2):
        whole.append(mirror(held, "seq", 2 * k))
    whole = tree_sum(whole)
    return whole, mirror(whole, "seq", 1)


def shards(tokens, cotangent, w_in, w_out, filter_taps, skip):
    width = w_out.shape[0]
    tok, cot = tokens[0], cotangent[0]
    rows = tok.shape[0]
    tiles = rows // LANES
    parts = lax.axis_size("seq")
    groups = lax.axis_size("dp")
    chans = width // parts
    share = parts // groups
    outer = parts * tiles
    chunk = min(chans, 32)
    size = tiles * chans
    half = width // groups // 2
    scale = 1.0 / math.sqrt(groups * parts * rows)
    first, last, twiddle, fwd, inv = tables(outer)
    place = None
    block = jax.ShapeDtypeStruct((parts // 2, size, LANES), F32)
    spectrum = jax.ShapeDtypeStruct((chans * outer, 2 * LANES), F32)
    signal = pltpu.VMEM((width, rows), F32)
    field = pltpu.VMEM((outer * chans, LANES), F32)
    split_rows = pltpu.VMEM((chunk * outer, 2 * LANES), BF16)
    n_blocks = parts // 2 + 1

    def taps_kernel(at_ref, taps_ref, keep_ref, give_ref, signal_ref):
        signal_ref[...] = taps_ref[...].T
        deal(at_ref[0], signal_ref, keep_ref, give_ref)

    taps_blocks = exchange(*call(taps_kernel, (place, filter_taps), (block, block), [signal]))

    def prep_kernel(at_ref, tok_ref, cot_ref, win_ref, wout_ref, *refs):
        signal_ref = refs[-1]
        gate_out, gate_in, values, dmixed = projections(tok_ref, cot_ref, win_ref, wout_ref)
        signal_ref[...] = values * gate_in
        deal(at_ref[0], signal_ref, *refs[:2])
        signal_ref[...] = dmixed * gate_out
        deal(at_ref[0], signal_ref, *refs[2:4])

    dealt = call(
        prep_kernel, (place, tok, cot, w_in, w_out), (block,) * 4, [signal],
        flops=8 * rows * width * width,
    )
    gated_blocks = exchange(*dealt[:2])
    dconv_blocks = exchange(*dealt[2:])

    work = chans * outer * LANES * 4 * (3 * 2 * LANES + 6 * outer)

    def split_blocks(refs):
        return refs[0], refs[1], refs[2:n_blocks]

    def loop(step):
        def body(index, carry):
            step(index * chunk, pl.ds(pl.multiple_of(index * chunk * outer, chunk * outer), chunk * outer))
            return carry

        lax.fori_loop(0, chans // chunk, body, 0)

    def taps_spectrum_kernel(at_ref, first_ref, tw_ref, fwd_ref, *refs):
        blocks, (h_ref, x_ref, zh_ref, zl_ref) = split_blocks(refs[:n_blocks]), refs[n_blocks:]
        collect(at_ref[0], x_ref, blocks)

        def step(base, span):
            h_ref[span, :] = forward(x_ref, base, chunk, chans, first_ref, tw_ref, fwd_ref, zh_ref, zl_ref)

        loop(step)

    (taps_spec,) = call(
        taps_spectrum_kernel, (place, first, twiddle, fwd, *taps_blocks), (spectrum,),
        [field, split_rows, split_rows], flops=work,
    )

    def conv_kernel(at_ref, first_ref, last_ref, tw_ref, fwd_ref, inv_ref, h_ref, *refs):
        blocks = split_blocks(refs[:n_blocks])
        g_ref, keep_ref, give_ref, x_ref, y_ref, zh_ref, zl_ref = refs[n_blocks:]
        collect(at_ref[0], x_ref, blocks)

        def step(base, span):
            g = forward(x_ref, base, chunk, chans, first_ref, tw_ref, fwd_ref, zh_ref, zl_ref)
            g_ref[span, :] = g
            product = multiply(halves(h_ref[span, :]), halves(g))
            inverse(product, y_ref, base, chunk, chans, last_ref, tw_ref, inv_ref)

        loop(step)
        deal_field(at_ref[0], y_ref, keep_ref, give_ref)

    gated_spec, conv_keep, conv_give = call(
        conv_kernel, (place, first, last, twiddle, fwd, inv, taps_spec, *gated_blocks),
        (spectrum, block, block), [field, field, split_rows, split_rows], flops=2 * work,
    )
    conv_blocks = exchange(conv_keep, conv_give)
    term = jax.ShapeDtypeStruct((groups, share * size, LANES), F32)

    def corr_kernel(at_ref, first_ref, last_ref, tw_ref, fwd_ref, inv_ref, h_ref, g_ref, *refs):
        blocks = split_blocks(refs[:n_blocks])
        keep_ref, give_ref, term_ref, x_ref, y_ref, k_ref, zh_ref, zl_ref = refs[n_blocks:]
        collect(at_ref[0], x_ref, blocks)

        def step(base, span):
            d = halves(forward(x_ref, base, chunk, chans, first_ref, tw_ref, fwd_ref, zh_ref, zl_ref))
            for spec_ref, field_ref in ((h_ref, y_ref), (g_ref, k_ref)):
                product = correlate(halves(spec_ref[span, :]), d)
                inverse(product, field_ref, base, chunk, chans, last_ref, tw_ref, inv_ref)

        loop(step)
        deal_field(at_ref[0], y_ref, keep_ref, give_ref)
        for k in range(groups):
            for v in range(share):
                dest = at_ref[1] ^ reversed_bits(k, groups)
                dest = dest ^ (at_ref[0] // share)
                row = (dest * share + ((at_ref[0] % share) ^ v)) * size
                term_ref[k, v * size : (v + 1) * size, :] = (
                    k_ref[pl.ds(pl.multiple_of(row, size), size), :] * scale
                )

    dgated_keep, dgated_give, term_parts = call(
        corr_kernel, (place, first, last, twiddle, fwd, inv, taps_spec, gated_spec, *dconv_blocks),
        (block, block, term), [field, field, field, split_rows, split_rows], flops=3 * work,
    )
    dgated_blocks = exchange(dgated_keep, dgated_give)

    def deal_part(at_ref, part_ref, keep_ref, give_ref):
        for k in range(groups):
            for flip, ref in enumerate((keep_ref, give_ref)):
                dest = at_ref[1] ^ reversed_bits(k, groups)
                start = (dest * 2 + ((at_ref[0] & 1) ^ flip)) * half
                ref[k] = part_ref[pl.ds(pl.multiple_of(start, half), half), :]

    def mix_kernel(at_ref, tok_ref, cot_ref, win_ref, wout_ref, skip_ref, *refs):
        blocks = split_blocks(refs[:n_blocks])
        mixed_ref, dproj_ref, keep_ref, give_ref, c_ref, part_ref = refs[n_blocks:]
        gate_out, gate_in, values, dmixed = projections(tok_ref, cot_ref, win_ref, wout_ref)
        gated = values * gate_in
        collect_signal(at_ref[0], c_ref, blocks)
        conv = c_ref[...] + skip_column(skip_ref, tiles) * gated
        mixed = (conv * gate_out).astype(BF16)
        dproj = (dmixed * conv).astype(BF16)
        dproj_ref[...] = dproj
        mixed_ref[...] = mixed
        part_ref[:, :width] = dot(tok_ref[...], dproj, ((0,), (1,))) * scale
        part_ref[:, width : 2 * width] = dot(mixed, cot_ref[...]) * scale
        product = dmixed * gate_out * gated * scale
        total = product[:, :LANES]
        for t in range(1, tiles):
            total = total + product[:, t * LANES : (t + 1) * LANES]
        part_ref[:, 2 * width :] = total
        deal_part(at_ref, part_ref, keep_ref, give_ref)

    early = 2 * width + LANES
    piece = jax.ShapeDtypeStruct((groups, half, early), F32)
    mixed, dproj_first, early_keep, early_give = call(
        mix_kernel, (place, tok, cot, w_in, w_out, skip[None, :], *conv_blocks),
        (jax.ShapeDtypeStruct((width, rows), BF16),) * 2 + (piece, piece),
        [signal, pltpu.VMEM((width, early), F32)], flops=14 * rows * width * width,
    )
    early_sum = reduce_rows(early_keep, early_give)

    def last_kernel(at_ref, tok_ref, cot_ref, win_ref, wout_ref, skip_ref, *refs):
        blocks = split_blocks(refs[:n_blocks])
        dproj_late_ref, keep_ref, give_ref, c_ref, part_ref = refs[n_blocks:]
        gate_out, gate_in, values, dmixed = projections(tok_ref, cot_ref, win_ref, wout_ref)
        collect_signal(at_ref[0], c_ref, blocks)
        dgated = c_ref[...] + skip_column(skip_ref, tiles) * (dmixed * gate_out)
        dproj = jnp.concatenate([(dgated * values).astype(BF16), (dgated * gate_in).astype(BF16)], axis=0)
        part_ref[...] = dot(tok_ref[...], dproj, ((0,), (1,))) * scale
        deal_part(at_ref, part_ref, keep_ref, give_ref)
        dproj_late_ref[...] = dproj

    piece = jax.ShapeDtypeStruct((groups, half, 2 * width), F32)
    dproj_late, late_keep, late_give = call(
        last_kernel, (place, tok, cot, w_in, w_out, skip[None, :], *dgated_blocks),
        (jax.ShapeDtypeStruct((2 * width, rows), BF16), piece, piece),
        [signal, pltpu.VMEM((width, 2 * width), F32)], flops=18 * rows * width * width,
    )

    def inputs_kernel(at_ref, win_ref, first_dproj_ref, late_dproj_ref, din_ref):
        dproj = jnp.concatenate([first_dproj_ref[...], late_dproj_ref[...]], axis=0)
        din_ref[...] = dot(dproj, win_ref[...], ((0,), (1,))).astype(BF16)

    (dinput,) = call(
        inputs_kernel, (place, w_in, dproj_first, dproj_late), (jax.ShapeDtypeStruct((rows, width), BF16),),
        flops=6 * rows * width * width,
    )

    def outputs_kernel(at_ref, wout_ref, mixed_ref, out_ref):
        out_ref[...] = dot(mixed_ref[...], wout_ref[...], ((0,), (0,))).astype(BF16)

    (output,) = call(
        outputs_kernel, (place, w_out, mixed), (jax.ShapeDtypeStruct((rows, width), BF16),),
        flops=2 * rows * width * width,
    )
    late_sum = reduce_rows(late_keep, late_give)

    grad_sum = spread_rows(jnp.concatenate([early_sum, late_sum], axis=1))
    term_sum = halve(term_parts)
    swap = [
        (i * parts + j, (j // share) * parts + (i ^ (j // share)) * share + j % share)
        for i in range(groups)
        for j in range(parts)
    ]
    term_sum = lax.ppermute(term_sum, ("dp", "seq"), swap)
    term_sum = term_sum.reshape(share, size, LANES)
    pieces = [term_sum] + [mirror(term_sum[k], "seq", k) for k in range(1, share)]

    def join_kernel(at_ref, *refs):
        sums, terms = refs[:2], refs[2 : 2 + share]
        in_ref, out_ref, taps_out_ref, skip_out_ref, skip_ref = refs[2 + share :]
        for flip, ref in enumerate(sums):
            row = pl.multiple_of(((at_ref[0] & 1) ^ flip) * half, half)
            span = pl.ds(row, half)
            in_ref[span, :width] = ref[:, :width]
            out_ref[span, :] = ref[:, width : 2 * width]
            skip_ref[span, :] = ref[:, 2 * width : early]
            in_ref[span, width:] = ref[:, early:]
        skip_out_ref[...] = jnp.sum(skip_ref[...], axis=1, keepdims=True).T
        for k in range(share):
            start = pl.multiple_of((k ^ (at_ref[0] % share)) * chans, chans)
            for t in range(tiles):
                span = slice(t * chans, (t + 1) * chans)
                piece = terms[k][span, :] if k else terms[0][0, span, :]
                taps_out_ref[pl.ds(start, chans), t * LANES : (t + 1) * LANES] = piece

    grad_in, grad_out, grad_taps, grad_skip = call(
        join_kernel, (place, *grad_sum, *pieces),
        (
            jax.ShapeDtypeStruct((2 * half, 3 * width), F32),
            jax.ShapeDtypeStruct((2 * half, width), F32),
            jax.ShapeDtypeStruct((share * chans, rows), F32),
            jax.ShapeDtypeStruct((1, 2 * half), F32),
        ),
        [pltpu.VMEM((2 * half, LANES), F32)], flops=rows * width,
    )
    return output[None], dinput[None], grad_in, grad_out, grad_taps.T, grad_skip[0]


def solution(mesh):
    return jax.shard_map(
        shards,
        mesh=mesh,
        in_specs=(P("dp", "seq", None), P("dp", "seq", None), P(), P(), P("seq", None), P()),
        out_specs=(
            P("dp", "seq", None),
            P("dp", "seq", None),
            P("dp", None),
            P("dp", None),
            P("seq", "dp"),
            P("dp"),
        ),
        check_vma=False,
    )
```
